512 devices in a mesh: seq: 64 (over z, x, core), exp: 8 (over y).
Axes of the slice: x: 4, y: 8, z: 8, core: 2. Of those that a mesh axis runs over, the one named last changes fastest.
Arguments:
- inner_x: bfloat16 [8192, 8192], P('seq', 'exp'), may hold values from -6 to 6
- inner_z: bfloat16 [8192, 8192], P('seq', 'exp'), may hold values from -6 to 6
- step_raw: bfloat16 [8192, 8192], P('seq', 'exp'), may hold values from -4.5 to 3
- conv_weight: float32 [4, 8192], P(None, 'exp'), may hold values from -3 to 3
- state_proj: bfloat16 [8192, 32], P('exp'), may hold values from -0.125 to 0.125
- step_bias: float32 [8192], P('exp'), may hold values from -7 to -2.3
- decay_log: float32 [16, 8192], P(None, 'exp'), may hold values from -4 to 2.8
- skip_gain: float32 [8192], P('exp'), may hold values from 0.5 to 1.5
- moe_tokens: bfloat16 [8192, 4096], P('seq', 'exp'), may hold values from -6 to 6
- routes: int32 [8192, 2], P('seq'), may hold values from 0 to 15, all different within a row; in each aligned block of 128 rows (0 to 127, 128 to 255, ...) at most 20 rows name the same one
- gate_weight: bfloat16 [8, 12288, 4096], P('exp', 'seq'), may hold values from -0.09375 to 0.09375
- up_weight: bfloat16 [8, 12288, 4096], P('exp', 'seq'), may hold values from -0.09375 to 0.09375
Outputs:
- mixed: bfloat16 [8192, 8192], P('seq', 'exp')
- hidden: bfloat16 [8, 12288, 1280], P('exp', 'seq')
The draws below stay inside these ranges and needn't reach their ends.
Inputs may be any that keep to these rules, and one draw needn't show every extreme that they name: `routes`: in each aligned block of 128 rows (the tokens of one device), no expert is named by more than 20 rows, a bound that some block reaches; the two choices of a token differ.
All inputs are finite; a program needn't handle non-finite values.
Results may differ from the reference program's by a relative error of at most 0.0051.
Values may be sent and summed in bfloat16 or wider, within the bound.
No kernel may reach another device: no remote copies, remote signals or barrier semaphores. Data moves between devices by JAX's collectives and lax.ppermute only.
A program may use at most 128 MiB of HBM per device.

```python
import math
import jax
import jax.numpy as jnp
import numpy as np
from jax import lax

D = 4096
E = 8192
STATE = 16
CONV = 4
EXPERTS = 16
TOP = 2
FF = 12288
TOK_DEV = 128
CAP = 20
FLIGHT = 8
TOKENS = 8192
N_SEQ = 64


def draw_step_raw(key, part):
    offset_key = jax.random.fold_in(key, 11)
    noise_key = jax.random.fold_in(key, 12)
    offset = jax.random.uniform(offset_key, (E,), jnp.float32, -2.5, 0.0)
    noise = 0.5 * jax.random.normal(noise_key, (TOKENS, E), jnp.float32)
    return jnp.clip(noise + offset[None, :], -4.5, 3.0).astype(jnp.bfloat16)


def block_levels(rng, extent, pieces, least, high):
    def one(position, shards_of):
        heights = jax.random.uniform(jax.random.fold_in(jax.random.fold_in(rng, 6), position), (shards_of,), jnp.float32, least / len(pieces), high / len(pieces))
        return jnp.repeat(jnp.exp(heights), extent[position] // shards_of).reshape((-1,) + (1,) * (len(extent) - position - 1))

    gain = one(*pieces[0])
    for cut in pieces[1:]:
        gain = gain * one(*cut)
    return gain


def deal_out(own_key, own, number, rows, number_of, top, most, lean):
    sequence = jax.random.permutation(own_key, number_of)
    packed, common = shares(number_of, rows * top, most, lean, True), shares(number_of, rows * top, most, lean, False)
    places = jnp.arange(number_of)

    def named(tallies, offset_by):
        used = int((tallies > 0).sum())
        fixed = max(1, used // 4)
        moved = fixed + (places - fixed + offset_by * (used - fixed)) % max(1, number_of - fixed)
        return jnp.zeros((number_of,), jnp.int32).at[sequence[jnp.where(places < fixed, places, moved)]].set(jnp.asarray(tallies, jnp.int32))

    tallies = jnp.where(number % 4 == 0, named(packed, number // 4), named(common, number - number // 4 - 1))
    mixed = jax.random.permutation(jax.random.fold_in(own, 3), number_of)
    source_of, sink = mixed[0:number_of // 2 * 2:2], mixed[1:number_of // 2 * 2:2]
    margin = jnp.minimum(tallies[source_of] - 1, most - tallies[sink]) // 2
    margin = jnp.where((source_of == sequence[0]) | (sink == sequence[0]) | (tallies[sink] == 0), 0, jnp.maximum(margin, 0))
    moved = jax.random.randint(jax.random.fold_in(own, 4), (number_of // 2,), 0, 1 << 20) % (margin + 1)
    tallies = tallies.at[source_of].add(-moved).at[sink].add(moved)
    labels = jnp.searchsorted(jnp.cumsum(tallies), jnp.arange(rows * top), side="right").astype(jnp.int32)
    grid = labels.reshape(top, rows).T
    grid = grid[jax.random.permutation(jax.random.fold_in(own, 1), rows)]
    offset_by = jax.random.randint(jax.random.fold_in(own, 2), (rows, 1), 0, top)
    return jnp.take_along_axis(grid, (jnp.arange(top)[None, :] + offset_by) % top, axis=1)


def shares(count, total, limit, slope, full):
    loads = [(1 << 20) // math.isqrt(standing ** slope) + 1 for standing in range(1, count + 1)]
    largest = limit if full else min(limit, max(-(-total // count), total * loads[0] // sum(loads)))
    least = 1 if total - largest >= count - 1 else 0
    given, spare = [largest] + [least] * (count - 1), total - largest - least * (count - 1)
    while spare > 0:
        free = [i for i in range(1, count) if given[i] < largest] or [i for i in range(1, count) if given[i] < limit]
        pool, budget = sum([loads[i] for i in free]), spare
        for i in free:
            extra = min(limit - given[i], max(1, budget * loads[i] // pool), spare)
            given[i] = given[i] + extra
            spare = spare - extra
    return np.array(given)


def bell_draw(rng, shape, deviation, reach, shards=(), kind=jnp.bfloat16):
    factor_of = block_levels(rng, shape, shards, -0.22, 0.18) if shards else 1.0
    entries = jax.random.normal(rng, shape, jnp.float32) * deviation * factor_of
    return jnp.minimum(jnp.maximum(entries, -reach), reach).astype(kind)


def setup_inputs(seed: int = 0) -> dict:
    key_of = jax.random.split(jax.random.key(seed), 13)
    inner_x = bell_draw(key_of[0], (TOKENS, E), 1.0, 6.0, ((0, 64), (1, 8)))
    inner_z = bell_draw(key_of[1], (TOKENS, E), 1.0, 6.0, ((0, 64), (1, 8)))
    step_raw = draw_step_raw(jax.random.fold_in(key_of[12], 71), 0)
    conv_weight = bell_draw(key_of[3], (CONV, E), CONV ** -0.5, 3.0, ((1, 8),), jnp.float32)
    state_proj = bell_draw(key_of[4], (E, 2 * STATE), (E // 4) ** -0.5, 0.125, ((0, 8),))
    step_bias = jnp.clip(-7.0 + 4.7 * jax.random.uniform(key_of[5], (E,), jnp.float32) ** block_levels(key_of[5], (E,), ((0, 8),), -0.2, 0.2), -7.0, -2.3)
    decay_log = jnp.clip(-4.0 + 6.8 * jax.random.uniform(key_of[6], (STATE, E), jnp.float32) ** block_levels(key_of[6], (STATE, E), ((1, 8),), -0.2, 0.2), -4.0, 2.8)
    skip_gain = jnp.clip(0.5 + 1.0 * jax.random.uniform(key_of[7], (E,), jnp.float32) ** block_levels(key_of[7], (E,), ((0, 8),), -0.2, 0.2), 0.5, 1.5)
    moe_tokens = bell_draw(key_of[8], (TOKENS, D), 1.0, 6.0, ((0, 64), (1, 8)))
    routes_keys = jax.random.split(jax.random.fold_in(key_of[9], 1), TOKENS // TOK_DEV)
    routes_turns = jax.random.permutation(jax.random.fold_in(key_of[9], 3), TOKENS // TOK_DEV)
    routes = jax.vmap(lambda own, number: deal_out(jax.random.fold_in(key_of[9], 2), own, number, TOK_DEV, EXPERTS, TOP, CAP, 2))(routes_keys, routes_turns).reshape((TOKENS, TOP))
    gate_weight = bell_draw(key_of[10], (FLIGHT, FF, D), D ** -0.5, 0.09375, ((0, 8), (1, 64)))
    up_weight = bell_draw(key_of[11], (FLIGHT, FF, D), D ** -0.5, 0.09375, ((0, 8), (1, 64)))
    return dict(inner_x=inner_x, inner_z=inner_z, step_raw=step_raw, conv_weight=conv_weight, state_proj=state_proj, step_bias=step_bias, decay_log=decay_log, skip_gain=skip_gain, moe_tokens=moe_tokens, routes=routes, gate_weight=gate_weight, up_weight=up_weight)


def expand_rows(slot_rows, gate_matrix, up_matrix):
    dims = (((1,), (1,)), ((), ()))
    gate_part = lax.dot_general(gate_matrix, slot_rows, dims, preferred_element_type=jnp.float32)
    up_part = lax.dot_general(up_matrix, slot_rows, dims, preferred_element_type=jnp.float32)
    return (jax.nn.silu(gate_part) * up_part).astype(jnp.bfloat16)


def slot_table(pair_ids, experts_count, capacity, tokens):
    onehot = (pair_ids[:, None] == jnp.arange(experts_count, dtype=jnp.int32)[None, :]).astype(jnp.int32)
    before = jnp.cumsum(onehot, axis=0) - onehot
    places = (before[:, :, None] == jnp.arange(capacity, dtype=jnp.int32)[None, None, :]).astype(jnp.int32)
    chosen = onehot[:, :, None] * places
    return jnp.sum(chosen.reshape(tokens, -1, experts_count * capacity), axis=1)


def mixer(inner_x, inner_z, step_raw, conv_weight, state_proj, step_bias, decay_log, skip_gain):
    length = inner_x.shape[0]
    taps = conv_weight.shape[0]
    widened = inner_x.astype(jnp.float32)
    padded = jnp.concatenate([jnp.zeros((taps - 1, widened.shape[1]), jnp.float32), widened], axis=0)
    conv_sum = jnp.zeros(widened.shape, jnp.float32)
    for offset in range(taps):
        conv_sum = conv_sum + conv_weight[offset][None, :] * padded[offset:offset + length]
    conv_out = jax.nn.silu(conv_sum)
    coeffs = jnp.dot(conv_out.astype(jnp.bfloat16), state_proj, preferred_element_type=jnp.float32)
    input_coef = coeffs[:, :STATE]
    output_coef = coeffs[:, STATE:]
    step_size = jax.nn.softplus(step_raw.astype(jnp.float32) + step_bias[None, :])
    rates = -jnp.exp(decay_log)

    def advance(state, row):
        step_row, in_row, out_row, conv_row = row
        state = jnp.exp(rates * step_row[None, :]) * state + in_row[:, None] * (step_row * conv_row)[None, :]
        return state, jnp.sum(out_row[:, None] * state, axis=0)

    start_state = jnp.zeros(rates.shape, jnp.float32)
    _, outputs = lax.scan(advance, start_state, (step_size, input_coef, output_coef, conv_out))
    result = (outputs + skip_gain[None, :] * conv_out) * jax.nn.silu(inner_z.astype(jnp.float32))
    return result.astype(jnp.bfloat16)


def expert_layer(moe_tokens, routes, gate_weight, up_weight):
    flight = gate_weight.shape[0]
    block_ids = routes.reshape(N_SEQ, TOK_DEV * TOP)
    block_rows = moe_tokens.reshape(N_SEQ, TOK_DEV, D)

    def dispatch(args):
        pair_ids, token_rows = args
        table = slot_table(pair_ids, flight, CAP, TOK_DEV)
        return jnp.dot(table.T.astype(jnp.bfloat16), token_rows, preferred_element_type=jnp.float32).astype(jnp.bfloat16)

    placed = lax.map(dispatch, (block_ids, block_rows))
    placed = placed.reshape(N_SEQ, flight, CAP, D).transpose(1, 0, 2, 3).reshape(flight, N_SEQ * CAP, D)

    def per_expert(args):
        slot_rows, gate_matrix, up_matrix = args
        return expand_rows(slot_rows, gate_matrix, up_matrix)

    return lax.map(per_expert, (placed, gate_weight, up_weight))


def reference(inner_x, inner_z, step_raw, conv_weight, state_proj, step_bias, decay_log, skip_gain, moe_tokens, routes, gate_weight, up_weight):
    mixed = mixer(inner_x, inner_z, step_raw, conv_weight, state_proj, step_bias, decay_log, skip_gain)
    hidden = expert_layer(moe_tokens, routes, gate_weight, up_weight)
    return (mixed, hidden)
```

```python
import functools

import jax
import jax.numpy as jnp
from jax import lax
from jax.experimental import pallas as pl
from jax.experimental.pallas import tpu as pltpu
from jax.sharding import Mesh
from jax.sharding import PartitionSpec as P

CAP = 20
F32 = jnp.float32
BF16 = jnp.bfloat16
LOG2E = 1.4426950408889634
SEQ = ("z", "x", "c")

VMEM = pl.BlockSpec(memory_space=pltpu.VMEM)
SMEM = pl.BlockSpec(memory_space=pltpu.SMEM)


def call(kernel, out_shape, in_specs, scratch=(), name=None):
    return pl.pallas_call(
        kernel,
        out_shape=out_shape,
        in_specs=in_specs,
        out_specs=jax.tree.map(lambda _: VMEM, out_shape),
        scratch_shapes=scratch,
        name=name,
        compiler_params=pltpu.CompilerParams(vmem_limit_bytes=48 << 20),
    )


def shape(dims, dtype):
    return jax.ShapeDtypeStruct(dims, dtype)


def place_kernel(routes_ref, tokens_ref, out_ref):
    rows = tokens_ref.shape[0]
    column = lax.broadcasted_iota(jnp.int32, (rows, 256), 1)
    expert, slot = column >> 5, column & 31
    named = (routes_ref[:, 0:1] == expert) | (routes_ref[:, 1:2] == expert)
    earlier = lax.broadcasted_iota(jnp.int32, (rows, rows), 0) > lax.broadcasted_iota(
        jnp.int32, (rows, rows), 1
    )
    before = jnp.dot(
        jnp.where(earlier, 1.0, 0.0).astype(BF16),
        jnp.where(named, 1.0, 0.0).astype(BF16),
        preferred_element_type=F32,
    )
    table = jnp.where(named & (before == slot.astype(F32)), 1.0, 0.0).astype(BF16)
    placed = lax.dot_general(
        table, tokens_ref[...], (((0,), (0,)), ((), ())), preferred_element_type=F32
    ).astype(BF16)
    for index in range(8):
        out_ref[index] = placed[index * 32 : index * 32 + CAP]


def silu(value):
    return value / (1.0 + jnp.exp(-value))


def softplus(value):
    small = jnp.exp(-jnp.abs(value))
    ratio = small / (2.0 + small)
    square = ratio * ratio
    series = jnp.full_like(square, 1.0 / 15.0)
    for odd in (13, 11, 9, 7, 5, 3):
        series = series * square + 1.0 / odd
    return jnp.maximum(value, 0.0) + 2.0 * ratio * (series * square + 1.0)


def conv_kernel(
    x_ref,
    rim_ref,
    raw_ref,
    weight_ref,
    proj_ref,
    bias_ref,
    decay_ref,
    conv_ref,
    step_ref,
    drive_ref,
    rate_ref,
    part_ref,
    padded,
):
    rows, width = x_ref.shape
    padded[8:, :] = x_ref[...].astype(F32)
    padded[5:8, :] = rim_ref[...].astype(F32)
    total = jnp.zeros((rows, width), F32)
    for tap in range(4):
        total = total + weight_ref[tap : tap + 1, :] * padded[5 + tap : 5 + tap + rows, :]
    conv = silu(total)
    conv_ref[...] = conv
    part = lax.dot_general(
        proj_ref[...], conv.astype(BF16), (((0,), (1,)), ((), ())), preferred_element_type=F32
    )
    for index in range(8):
        part_ref[index] = part
    step = softplus(raw_ref[...].astype(F32) + bias_ref[...])
    drive = step * conv
    rate = -jnp.exp(decay_ref[...]) * LOG2E
    for index in range(width // 128):
        lanes = slice(index * 128, index * 128 + 128)
        step_ref[pl.ds(index, rows, stride=8), :] = step[:, lanes]
        drive_ref[pl.ds(index, rows, stride=8), :] = drive[:, lanes]
        rate_ref[pl.ds(index, rate.shape[0], stride=8), :] = rate[:, lanes]


def pack_state(states, total):
    high = total.astype(BF16).astype(F32)
    middle = (total - high).astype(BF16).astype(F32)
    low = total - high - middle
    tail = jnp.concatenate([high, middle, low, jnp.zeros_like(total)], axis=0)
    return jnp.concatenate(list(states) + [tail], axis=0).astype(BF16)


def unpack_state(ref, position):
    block = ref[position].astype(F32)
    states = [block[n * 8 : n * 8 + 8] for n in range(16)]
    return states, block[128:136] + block[136:144] + block[144:152]


def scan_kernel(coef_ref, step_ref, drive_ref, rate_ref, y_ref, sum_ref, end_ref):
    rows = step_ref.shape[0] // 8
    rates = [rate_ref[n * 8 : n * 8 + 8, :] for n in range(16)]
    zero = jnp.zeros((8, 128), F32)

    def advance(token, carry):
        total, states = carry
        here = pl.ds(pl.multiple_of(token * 8, 8), 8)
        step, drive = step_ref[here, :], drive_ref[here, :]
        total = total + step
        sum_ref[here, :] = total
        parts, following = [zero, zero], []
        for n in range(16):
            state = jnp.exp2(rates[n] * step) * states[n] + coef_ref[n, token] * drive
            parts[n % 2] = parts[n % 2] + coef_ref[16 + n, token] * state
            following.append(state)
        y_ref[here, :] = parts[0] + parts[1]
        return total, tuple(following)

    total, states = lax.fori_loop(0, rows, advance, (zero, (zero,) * 16), unroll=4)
    packed = pack_state(states, total)
    for index in range(8):
        end_ref[index] = packed


def fold(ref, rates, limit, states, total):
    for position in range(8):
        more, step = unpack_state(ref, position)
        keep = position < limit
        states = [
            jnp.where(keep, jnp.exp2(rates[n] * step) * states[n] + more[n], states[n])
            for n in range(16)
        ]
        total = jnp.where(keep, total + step, total)
    return states, total


def group_kernel(mine_ref, got_ref, rate_ref, before_ref, step_ref, all_ref):
    rates = [rate_ref[n * 8 : n * 8 + 8, :] for n in range(16)]
    zero = jnp.zeros((8, 128), F32)
    states, total = fold(got_ref, rates, mine_ref[0], [zero] * 16, zero)
    for n in range(16):
        before_ref[n * 8 : n * 8 + 8, :] = states[n]
    step_ref[...] = total
    states, total = fold(got_ref, rates, 8, [zero] * 16, zero)
    packed = pack_state(states, total)
    for index in range(8):
        all_ref[index] = packed


def finish_kernel(
    mine_ref,
    coef_ref,
    got_ref,
    rate_ref,
    before_ref,
    before_step_ref,
    y_ref,
    sum_ref,
    conv_ref,
    gain_ref,
    z_ref,
    out_ref,
    dense,
):
    rows, width = conv_ref.shape
    rates = [rate_ref[n * 8 : n * 8 + 8, :] for n in range(16)]
    zero = jnp.zeros((8, 128), F32)
    states, _ = fold(got_ref, rates, mine_ref[0], [zero] * 16, zero)
    states = [
        jnp.exp2(rates[n] * before_step_ref[...]) * states[n] + before_ref[n * 8 : n * 8 + 8, :]
        for n in range(16)
    ]

    def advance(token, carry):
        here = pl.ds(pl.multiple_of(token * 8, 8), 8)
        total = sum_ref[here, :]
        parts = [y_ref[here, :], zero]
        for n in range(16):
            parts[n % 2] = parts[n % 2] + coef_ref[16 + n, token] * (
                jnp.exp2(rates[n] * total) * states[n]
            )
        dense[here, :] = parts[0] + parts[1]
        return carry

    lax.fori_loop(0, rows, advance, 0, unroll=4)
    for index in range(width // 128):
        lanes = slice(index * 128, index * 128 + 128)
        value = dense[pl.ds(index, rows, stride=8), :]
        value = value + gain_ref[:, lanes] * conv_ref[:, lanes]
        out_ref[:, lanes] = (value * silu(z_ref[:, lanes].astype(F32))).astype(BF16)


def expand_rows(slot_rows, gate_matrix, up_matrix):
    dims = (((1,), (1,)), ((), ()))
    gate_part = lax.dot_general(gate_matrix, slot_rows, dims, preferred_element_type=F32)
    up_part = lax.dot_general(up_matrix, slot_rows, dims, preferred_element_type=F32)
    return (jax.nn.silu(gate_part) * up_part).astype(BF16)


def shards(
    inner_x,
    inner_z,
    step_raw,
    conv_weight,
    state_proj,
    step_bias,
    decay_log,
    skip_gain,
    moe_tokens,
    routes,
    gate_weight,
    up_weight,
):
    rows, width = inner_x.shape
    shards_of = lax.axis_size(SEQ)
    rim = lax.ppermute(inner_x[rows - 3 :], SEQ, [(i, i + 1) for i in range(shards_of - 1)])
    placed = call(place_kernel, shape((8, CAP, moe_tokens.shape[1]), BF16), [VMEM] * 2, name="place")(
        routes, moe_tokens
    )
    arrived = lax.all_to_all(placed, "exp", split_axis=0, concat_axis=2, tiled=True)
    gathered = lax.all_gather(arrived[0], SEQ, axis=0, tiled=True)

    dense = shape((rows * width // 128, 128), F32)
    conv, step, drive, rate, part = call(
        conv_kernel,
        (
            shape((rows, width), F32),
            dense,
            dense,
            shape((128, 128), F32),
            shape((8, 32, rows), F32),
        ),
        [VMEM] * 7,
        [pltpu.VMEM((rows + 8, width), F32)],
        name="conv",
    )(inner_x, rim, step_raw, conv_weight, state_proj, step_bias[None], decay_log)
    coef = jnp.sum(lax.all_to_all(part, "exp", split_axis=0, concat_axis=0, tiled=True), axis=0)
    packed = shape((8, 160, 128), BF16)
    local, sums, ends = call(
        scan_kernel, (dense, dense, packed), [SMEM] + [VMEM] * 3, name="scan"
    )(coef, step, drive, rate)
    near = lax.all_to_all(ends, ("x", "c"), split_axis=0, concat_axis=0, tiled=True)
    place_in = lax.axis_index(("x", "c")).astype(jnp.int32).reshape(1)
    before, before_step, whole = call(
        group_kernel,
        (shape((128, 128), F32), shape((8, 128), F32), packed),
        [SMEM, VMEM, VMEM],
        name="group",
    )(place_in, near, rate)
    far = lax.all_to_all(whole, "z", split_axis=0, concat_axis=0, tiled=True)
    layer = lax.axis_index("z").astype(jnp.int32).reshape(1)
    mixed = call(
        finish_kernel,
        shape((rows, width), BF16),
        [SMEM, SMEM] + [VMEM] * 9,
        [pltpu.VMEM(dense.shape, F32)],
        name="finish",
    )(layer, coef, far, rate, before, before_step, local, sums, conv, skip_gain[None], inner_z)

    hidden = expand_rows(gathered, gate_weight[0], up_weight[0])[None]
    return mixed, hidden


def solution(mesh):
    fine = Mesh(mesh.devices.reshape(8, 4, 2, 8), ("z", "x", "c", "exp"))
    return jax.shard_map(
        shards,
        mesh=fine,
        in_specs=(
            P(SEQ, "exp"),
            P(SEQ, "exp"),
            P(SEQ, "exp"),
            P(None, "exp"),
            P("exp", None),
            P("exp"),
            P(None, "exp"),
            P("exp"),
            P(SEQ, "exp"),
            P(SEQ, None),
            P("exp", SEQ, None),
            P("exp", SEQ, None),
        ),
        out_specs=(P(SEQ, "exp"), P("exp", SEQ, None)),
        check_vma=False,
    )
```

```python
import functools

import jax
import jax.numpy as jnp
from jax import lax
from jax.experimental import pallas as pl
from jax.experimental.pallas import tpu as pltpu
from jax.sharding import Mesh
from jax.sharding import PartitionSpec as P

CAP = 20
F32 = jnp.float32
BF16 = jnp.bfloat16
LOG2E = 1.4426950408889634
SEQ = ("z", "x", "c")

FIRST = 12
REST = CAP - FIRST

VMEM = pl.BlockSpec(memory_space=pltpu.VMEM)
SMEM = pl.BlockSpec(memory_space=pltpu.SMEM)


def call(kernel, out_shape, in_specs, scratch=(), name=None, vmem=16, flops=0):
    return pl.pallas_call(
        kernel,
        out_shape=out_shape,
        in_specs=in_specs,
        out_specs=jax.tree.map(lambda _: VMEM, out_shape),
        scratch_shapes=scratch,
        name=name,
        compiler_params=pltpu.CompilerParams(vmem_limit_bytes=vmem << 20),
        cost_estimate=pl.CostEstimate(flops=flops, transcendentals=0, bytes_accessed=4 << 20),
    )


def shape(dims, dtype):
    return jax.ShapeDtypeStruct(dims, dtype)


def place_kernel(routes_ref, tokens_ref, first_ref, rest_ref):
    rows = tokens_ref.shape[0]
    column = lax.broadcasted_iota(jnp.int32, (rows, 256), 1)
    expert, slot = column >> 5, column & 31
    slot = jnp.where(slot < 16, slot, slot - 16 + FIRST)
    named = (routes_ref[:, 0:1] == expert) | (routes_ref[:, 1:2] == expert)
    earlier = lax.broadcasted_iota(jnp.int32, (rows, rows), 0) > lax.broadcasted_iota(
        jnp.int32, (rows, rows), 1
    )
    before = jnp.dot(
        jnp.where(earlier, 1.0, 0.0).astype(BF16),
        jnp.where(named, 1.0, 0.0).astype(BF16),
        preferred_element_type=F32,
    )
    table = jnp.where(named & (before == slot.astype(F32)), 1.0, 0.0).astype(BF16)
    placed = lax.dot_general(
        table, tokens_ref[...], (((0,), (0,)), ((), ())), preferred_element_type=F32
    ).astype(BF16)
    for index in range(8):
        start = index * 32
        for copy in range(4):
            first_ref[index * 4 + copy] = placed[start : start + FIRST]
        for copy in range(8):
            rest_ref[index * 8 + copy] = placed[start + 16 : start + 16 + REST]


def assemble_kernel(got_ref, out_ref, wide):
    slots = got_ref.shape[1]
    peers = got_ref.shape[0] // 8
    for block in range(8):
        for peer in range(peers):
            wide[peer * slots : peer * slots + slots, block * 512 : block * 512 + 512] = got_ref[
                block * peers + peer
            ].astype(F32)
    out_ref[...] = wide[...].astype(BF16)


def assemble(got, name):
    dims = (got.shape[0] // 8 * got.shape[1], 4096)
    return call(
        assemble_kernel, shape(dims, BF16), [VMEM], [pltpu.VMEM(dims, F32)], name=name, flops=1 << 28
    )(got)


def expand_kernel(gate_ref, up_ref, other_gate_ref, other_up_ref, *refs):
    dims = (((1,), (1,)), ((), ()))
    rows_refs, out_refs = refs[:-2], refs[-2:]
    pairs = ((gate_ref, up_ref), (other_gate_ref, other_up_ref))
    for (gate, up), out_ref in zip(pairs, out_refs):
        start = 0
        for rows_ref in rows_refs:
            count = rows_ref.shape[0]
            rows = rows_ref[...]
            gated = lax.dot_general(gate[...], rows, dims, preferred_element_type=F32)
            upped = lax.dot_general(up[...], rows, dims, preferred_element_type=F32)
            out_ref[:, start : start + count] = (silu(gated) * upped).astype(BF16)
            start += count


def expand(weights, blocks, name):
    units, rows = weights[0].shape[0], sum(block.shape[0] for block in blocks)
    return call(
        expand_kernel,
        (shape((units, rows), BF16),) * 2,
        [VMEM] * (4 + len(blocks)),
        name=name,
        vmem=32,
        flops=8 * units * rows * 4096,
    )(*weights, *blocks)


def order_kernel(x_ref, core_ref, first_ref, rest_ref, other_first_ref, other_rest_ref, out_ref):
    columns = out_ref.shape[1]
    total = jnp.zeros(out_ref.shape, F32)
    sets = ((first_ref, rest_ref, core_ref[0]), (other_first_ref, other_rest_ref, 1 - core_ref[0]))
    for early_ref, late_ref, core in sets:
        for ref in (early_ref, late_ref):
            count = ref.shape[1]
            row = lax.broadcasted_iota(jnp.int32, (count, 1), 0)
            if ref is early_ref:
                layer, rest = row // (4 * FIRST), row % (4 * FIRST)
                across, slot = rest // FIRST, rest % FIRST
            else:
                block, rest = row // (8 * REST), row % (8 * REST)
                layer, slot = rest // REST, rest % REST + FIRST
                shift = jnp.where(block == 0, 0, jnp.where(block == 1, 3, jnp.where(block == 2, 1, 2)))
                across = (x_ref[0] + shift) & 3
            column = ((layer * 4 + across) * 2 + core) * CAP + slot
            table = lax.broadcasted_iota(jnp.int32, (count, columns), 1) == column
            total = total + jnp.dot(
                ref[...], jnp.where(table, 1.0, 0.0).astype(BF16), preferred_element_type=F32
            )
    out_ref[...] = total.astype(BF16)


def silu(value):
    return value / (1.0 + jnp.exp(-value))


def softplus(value):
    small = jnp.exp(-jnp.abs(value))
    ratio = small / (2.0 + small)
    square = ratio * ratio
    series = jnp.full_like(square, 1.0 / 15.0)
    for odd in (13, 11, 9, 7, 5, 3):
        series = series * square + 1.0 / odd
    return jnp.maximum(value, 0.0) + 2.0 * ratio * (series * square + 1.0)


def conv_kernel(
    x_ref,
    rim_ref,
    raw_ref,
    weight_ref,
    proj_ref,
    bias_ref,
    decay_ref,
    conv_ref,
    step_ref,
    drive_ref,
    rate_ref,
    part_ref,
    padded,
):
    rows, width = x_ref.shape
    padded[8:, :] = x_ref[...].astype(F32)
    padded[5:8, :] = rim_ref[...].astype(F32)
    total = jnp.zeros((rows, width), F32)
    for tap in range(4):
        total = total + weight_ref[tap : tap + 1, :] * padded[5 + tap : 5 + tap + rows, :]
    conv = silu(total)
    conv_ref[...] = conv
    part = lax.dot_general(
        proj_ref[...], conv.astype(BF16), (((0,), (1,)), ((), ())), preferred_element_type=F32
    )
    for index in range(8):
        part_ref[index] = part
    step = softplus(raw_ref[...].astype(F32) + bias_ref[...])
    drive = step * conv
    rate = -jnp.exp(decay_ref[...]) * LOG2E
    for index in range(width // 128):
        lanes = slice(index * 128, index * 128 + 128)
        step_ref[pl.ds(index, rows, stride=8), :] = step[:, lanes]
        drive_ref[pl.ds(index, rows, stride=8), :] = drive[:, lanes]
        rate_ref[pl.ds(index, rate.shape[0], stride=8), :] = rate[:, lanes]


def pack_state(states, total):
    high = total.astype(BF16).astype(F32)
    middle = (total - high).astype(BF16).astype(F32)
    low = total - high - middle
    tail = jnp.concatenate([high, middle, low, jnp.zeros_like(total)], axis=0)
    return jnp.concatenate(list(states) + [tail], axis=0).astype(BF16)


def unpack_state(ref, position):
    block = ref[position].astype(F32)
    states = [block[n * 8 : n * 8 + 8] for n in range(16)]
    return states, block[128:136] + block[136:144] + block[144:152]


def scan_kernel(coef_ref, step_ref, drive_ref, rate_ref, y_ref, sum_ref, end_ref):
    rows = step_ref.shape[0] // 8
    rates = [rate_ref[n * 8 : n * 8 + 8, :] for n in range(16)]
    zero = jnp.zeros((8, 128), F32)

    def advance(token, carry):
        total, states = carry
        here = pl.ds(pl.multiple_of(token * 8, 8), 8)
        step, drive = step_ref[here, :], drive_ref[here, :]
        total = total + step
        sum_ref[here, :] = total
        parts, following = [zero, zero], []
        for n in range(16):
            state = jnp.exp2(rates[n] * step) * states[n] + coef_ref[n, token] * drive
            parts[n % 2] = parts[n % 2] + coef_ref[16 + n, token] * state
            following.append(state)
        y_ref[here, :] = parts[0] + parts[1]
        return total, tuple(following)

    total, states = lax.fori_loop(0, rows, advance, (zero, (zero,) * 16), unroll=4)
    packed = pack_state(states, total)
    for index in range(8):
        end_ref[index] = packed


def fold(ref, rates, limit, states, total):
    for position in range(8):
        more, step = unpack_state(ref, position)
        keep = position < limit
        states = [
            jnp.where(keep, jnp.exp2(rates[n] * step) * states[n] + more[n], states[n])
            for n in range(16)
        ]
        total = jnp.where(keep, total + step, total)
    return states, total


def group_kernel(mine_ref, got_ref, rate_ref, before_ref, step_ref, all_ref):
    rates = [rate_ref[n * 8 : n * 8 + 8, :] for n in range(16)]
    zero = jnp.zeros((8, 128), F32)
    states, total = fold(got_ref, rates, mine_ref[0], [zero] * 16, zero)
    for n in range(16):
        before_ref[n * 8 : n * 8 + 8, :] = states[n]
    step_ref[...] = total
    states, total = fold(got_ref, rates, 8, [zero] * 16, zero)
    packed = pack_state(states, total)
    for index in range(8):
        all_ref[index] = packed


def finish_kernel(
    mine_ref,
    coef_ref,
    got_ref,
    rate_ref,
    before_ref,
    before_step_ref,
    y_ref,
    sum_ref,
    conv_ref,
    gain_ref,
    z_ref,
    out_ref,
    dense,
):
    rows, width = conv_ref.shape
    rates = [rate_ref[n * 8 : n * 8 + 8, :] for n in range(16)]
    zero = jnp.zeros((8, 128), F32)
    states, _ = fold(got_ref, rates, mine_ref[0], [zero] * 16, zero)
    states = [
        jnp.exp2(rates[n] * before_step_ref[...]) * states[n] + before_ref[n * 8 : n * 8 + 8, :]
        for n in range(16)
    ]

    def advance(token, carry):
        here = pl.ds(pl.multiple_of(token * 8, 8), 8)
        total = sum_ref[here, :]
        parts = [y_ref[here, :], zero]
        for n in range(16):
            parts[n % 2] = parts[n % 2] + coef_ref[16 + n, token] * (
                jnp.exp2(rates[n] * total) * states[n]
            )
        dense[here, :] = parts[0] + parts[1]
        return carry

    lax.fori_loop(0, rows, advance, 0, unroll=4)
    for index in range(width // 128):
        lanes = slice(index * 128, index * 128 + 128)
        value = dense[pl.ds(index, rows, stride=8), :]
        value = value + gain_ref[:, lanes] * conv_ref[:, lanes]
        out_ref[:, lanes] = (value * silu(z_ref[:, lanes].astype(F32))).astype(BF16)


def shards(
    inner_x,
    inner_z,
    step_raw,
    conv_weight,
    state_proj,
    step_bias,
    decay_log,
    skip_gain,
    moe_tokens,
    routes,
    gate_weight,
    up_weight,
):
    rows, width = inner_x.shape
    shards_of = lax.axis_size(SEQ)
    rim = lax.ppermute(inner_x[rows - 3 :], SEQ, [(i, i + 1) for i in range(shards_of - 1)])
    swap, ahead, back = [(0, 1), (1, 0)], *([(i, (i + d) % 4) for i in range(4)] for d in (1, 3))
    features = moe_tokens.shape[1]
    first, rest = call(
        place_kernel,
        (shape((32, FIRST, features), BF16), shape((64, REST, features), BF16)),
        [VMEM] * 2,
        name="place",
        flops=1 << 28,
    )(routes, moe_tokens)
    first = lax.all_to_all(first, ("exp", "x"), split_axis=0, concat_axis=0, tiled=True)
    rest = lax.all_to_all(rest, ("exp", "z"), split_axis=0, concat_axis=0, tiled=True)
    first = lax.all_gather(assemble(first, "assemble_first"), "z", axis=0, tiled=True)
    rest = assemble(rest, "assemble_rest")
    half = rest.shape[0] // 2
    left = lax.ppermute(rest, "x", ahead)
    right = lax.ppermute(rest, "x", back)
    far_left = lax.ppermute(left[:half], "x", ahead)
    far_right = lax.ppermute(right[half:], "x", back)
    weights = [gate_weight[0], up_weight[0]]
    weights = weights + [lax.ppermute(weight, "c", swap) for weight in weights]

    dense = shape((rows * width // 128, 128), F32)
    conv, step, drive, rate, part = call(
        conv_kernel,
        (
            shape((rows, width), F32),
            dense,
            dense,
            shape((128, 128), F32),
            shape((8, 32, rows), F32),
        ),
        [VMEM] * 7,
        [pltpu.VMEM((rows + 8, width), F32)],
        name="conv", flops=1 << 29,
    )(inner_x, rim, step_raw, conv_weight, state_proj, step_bias[None], decay_log)
    coef = jnp.sum(lax.all_to_all(part, "exp", split_axis=0, concat_axis=0, tiled=True), axis=0)
    packed = shape((8, 160, 128), BF16)
    local, sums, ends = call(
        scan_kernel, (dense, dense, packed), [SMEM] + [VMEM] * 3, name="scan", flops=1 << 31
    )(coef, step, drive, rate)
    near = lax.all_to_all(ends, ("x", "c"), split_axis=0, concat_axis=0, tiled=True)
    place_in = lax.axis_index(("x", "c")).astype(jnp.int32).reshape(1)
    before, before_step, whole = call(
        group_kernel,
        (shape((128, 128), F32), shape((8, 128), F32), packed),
        [SMEM, VMEM, VMEM],
        name="group", flops=1 << 28,
    )(place_in, near, rate)
    far = lax.all_to_all(whole, "z", split_axis=0, concat_axis=0, tiled=True)
    layer = lax.axis_index("z").astype(jnp.int32).reshape(1)
    mixed = call(
        finish_kernel,
        shape((rows, width), BF16),
        [SMEM, SMEM] + [VMEM] * 9,
        [pltpu.VMEM(dense.shape, F32)],
        name="finish", flops=1 << 31,
    )(layer, coef, far, rate, before, before_step, local, sums, conv, skip_gain[None], inner_z)

    mine_rest, theirs_rest = expand(weights, [rest, left, right, far_left, far_right], "expand_rest")
    mine, theirs = expand(weights, [first], "expand_first")
    other_rest = lax.ppermute(theirs_rest, "c", swap)
    other = lax.ppermute(theirs, "c", swap)
    here = [lax.axis_index(axis).astype(jnp.int32).reshape(1) for axis in ("x", "c")]
    units = gate_weight.shape[1]
    hidden = call(
        order_kernel,
        shape((units, 1280), BF16),
        [SMEM, SMEM] + [VMEM] * 4,
        name="order",
        flops=1 << 28,
    )(*here, mine, mine_rest, other, other_rest)[None]
    return mixed, hidden


def solution(mesh):
    fine = Mesh(mesh.devices.reshape(8, 4, 2, 8), ("z", "x", "c", "exp"))
    return jax.shard_map(
        shards,
        mesh=fine,
        in_specs=(
            P(SEQ, "exp"),
            P(SEQ, "exp"),
            P(SEQ, "exp"),
            P(None, "exp"),
            P("exp", None),
            P("exp"),
            P(None, "exp"),
            P("exp"),
            P(SEQ, "exp"),
            P(SEQ, None),
            P("exp", SEQ, None),
            P("exp", SEQ, None),
        ),
        out_specs=(P(SEQ, "exp"), P("exp", SEQ, None)),
        check_vma=False,
    )
```

```python
import functools

import jax
import jax.numpy as jnp
from jax import lax
from jax.experimental import pallas as pl
from jax.experimental.pallas import tpu as pltpu
from jax.sharding import Mesh
from jax.sharding import PartitionSpec as P

CAP = 20
F32 = jnp.float32
BF16 = jnp.bfloat16
LOG2E = 1.4426950408889634
SEQ = ("z", "x", "c")

FIRST = 12
REST = CAP - FIRST

VMEM = pl.BlockSpec(memory_space=pltpu.VMEM)
SMEM = pl.BlockSpec(memory_space=pltpu.SMEM)
WHOLE = pl.BlockSpec(memory_space=pltpu.HBM)


def call(kernel, out_shape, in_specs, scratch=(), name=None, vmem=60, flops=0, lazy=False, stack=0):
    single = not isinstance(out_shape, tuple)
    outs = (out_shape,) if single else out_shape

    def run(*operands):
        moved = [index for index in range(stack, len(in_specs)) if in_specs[index] is WHOLE]
        buffers = [pltpu.VMEM(operands[index].shape, operands[index].dtype) for index in moved]
        buffers += [pltpu.VMEM(out.shape, out.dtype) for out in outs]
        sizes = [operand.shape[0] for operand in operands[:stack]]
        if stack:
            buffers.append(pltpu.VMEM((sum(sizes),) + operands[0].shape[1:], operands[0].dtype))
        count = len(operands)

        def body(*refs):
            inputs, results = list(refs[:count]), refs[count : count + len(outs)]
            held = refs[count + len(outs) : count + len(outs) + len(buffers)]
            rest, sems = refs[count + len(outs) + len(buffers) : -1], refs[-1]
            copies = []
            for place, index in enumerate(moved):
                copies.append(pltpu.make_async_copy(inputs[index], held[place], sems.at[place]))
                inputs[index] = held[place]
            for place, size in enumerate(sizes):
                target = held[-1].at[pl.ds(sum(sizes[:place]), size)]
                copies.append(
                    pltpu.make_async_copy(inputs[place], target, sems.at[len(buffers) + place])
                )
            for copy in copies:
                copy.start()
            if stack:
                inputs = [held[-1]] + inputs[stack:]
            made = held[len(moved) : len(moved) + len(outs)]
            if lazy:
                kernel(copies, *inputs, *made, *rest)
            else:
                for copy in copies:
                    copy.wait()
                kernel(*inputs, *made, *rest)
            copies = [
                pltpu.make_async_copy(source, target, sems.at[len(moved) + place])
                for place, (source, target) in enumerate(zip(made, results))
            ]
            for copy in copies:
                copy.start()
            for copy in copies:
                copy.wait()

        found = pl.pallas_call(
            body,
            out_shape=outs,
            in_specs=in_specs,
            out_specs=(WHOLE,) * len(outs),
            scratch_shapes=[*buffers, *scratch, pltpu.SemaphoreType.DMA((len(buffers) + stack,))],
            name=name,
            compiler_params=pltpu.CompilerParams(vmem_limit_bytes=vmem << 20),
            cost_estimate=pl.CostEstimate(flops=flops, transcendentals=0, bytes_accessed=4 << 20),
        )(*operands)
        return found[0] if single else found

    return run


def shape(dims, dtype):
    return jax.ShapeDtypeStruct(dims, dtype)


def place_kernel(routes_ref, tokens_ref, out_ref):
    rows = tokens_ref.shape[0]
    column = lax.broadcasted_iota(jnp.int32, (rows, 256), 1)
    expert, slot = column >> 5, column & 31
    named = (routes_ref[:, 0:1] == expert) | (routes_ref[:, 1:2] == expert)
    earlier = lax.broadcasted_iota(jnp.int32, (rows, rows), 0) > lax.broadcasted_iota(
        jnp.int32, (rows, rows), 1
    )
    before = jnp.dot(
        jnp.where(earlier, 1.0, 0.0).astype(BF16),
        jnp.where(named, 1.0, 0.0).astype(BF16),
        preferred_element_type=F32,
    )
    table = jnp.where(named & (before == slot.astype(F32)), 1.0, 0.0).astype(BF16)
    placed = lax.dot_general(
        table, tokens_ref[...], (((0,), (0,)), ((), ())), preferred_element_type=F32
    ).astype(BF16)
    for index in range(8):
        out_ref[index] = placed[index * 32 : index * 32 + CAP]


def unpack_kernel(got_ref, first_ref, rest_ref, wide):
    for block in range(8):
        wide[:, block * 512 : block * 512 + 512] = got_ref[block].astype(F32)
    first_ref[...] = wide[:FIRST].astype(BF16)
    rest = wide[FIRST:].astype(BF16)
    for copy in range(8):
        rest_ref[copy] = rest


def join_kernel(*refs):
    parts, out_ref, wide = refs[:-2], refs[-2], refs[-1]
    for index, ref in enumerate(parts):
        wide[index * FIRST : index * FIRST + FIRST, :] = ref[...].astype(F32)
    out_ref[...] = wide[...].astype(BF16)


def expand_kernel(copies, rows_ref, other_ref, weight_ref, other_out_ref, out_ref):
    dims = (((1,), (1,)), ((), ()))
    units = out_ref.shape[0]
    for copy in copies[2:]:
        copy.wait()
    sets = ((copies[0], other_ref, other_out_ref), (copies[1], weight_ref, out_ref))
    for copy, weight, out in sets:
        copy.wait()
        both = lax.dot_general(weight[...], rows_ref[...], dims, preferred_element_type=F32)
        out[...] = (silu(both[:units]) * both[units:]).astype(BF16)


def expand(weights, blocks, name):
    units, count = weights[0].shape[0] // 2, sum(block.shape[0] for block in blocks)
    return call(
        expand_kernel,
        (shape((units, count), BF16),) * 2,
        [WHOLE] * (2 + len(blocks)),
        name=name,
        flops=8 * units * count * 4096,
        lazy=True,
        stack=len(blocks),
    )(*blocks, weights[1], weights[0])


def divided(value, by):
    return (value * (65536 // by + 1)) >> 16


def order_kernel(x_ref, core_ref, first_ref, rest_ref, other_first_ref, other_rest_ref, out_ref):
    columns = out_ref.shape[1]
    total = jnp.zeros(out_ref.shape, F32)
    sets = ((first_ref, rest_ref, core_ref[0]), (other_first_ref, other_rest_ref, 1 - core_ref[0]))
    for early_ref, late_ref, core in sets:
        for ref in (early_ref, late_ref):
            count = ref.shape[1]
            row = lax.broadcasted_iota(jnp.int32, (count, 1), 0)
            if ref is early_ref:
                block = divided(row, FIRST)
                slot = row - block * FIRST
                layer, near = block >> 2, block & 3
            else:
                block = divided(row, REST)
                slot = row - block * REST + FIRST
                layer, near = block & 7, block >> 3
            across = (x_ref[0] + jnp.where(near == 0, 0, jnp.where(near == 1, 3, near - 1))) & 3
            column = ((layer * 4 + across) * 2 + core) * CAP + slot
            table = lax.broadcasted_iota(jnp.int32, (count, columns), 1) == column
            total = total + jnp.dot(
                ref[...], jnp.where(table, 1.0, 0.0).astype(BF16), preferred_element_type=F32
            )
    out_ref[...] = total.astype(BF16)


def silu(value):
    return value / (1.0 + jnp.exp(-value))


def softplus(value):
    small = jnp.exp(-jnp.abs(value))
    ratio = small / (2.0 + small)
    square = ratio * ratio
    series = jnp.full_like(square, 1.0 / 15.0)
    for odd in (13, 11, 9, 7, 5, 3):
        series = series * square + 1.0 / odd
    return jnp.maximum(value, 0.0) + 2.0 * ratio * (series * square + 1.0)


def conv_kernel(
    x_ref,
    rim_ref,
    raw_ref,
    weight_ref,
    proj_ref,
    bias_ref,
    decay_ref,
    conv_ref,
    step_ref,
    drive_ref,
    rate_ref,
    part_ref,
    padded,
):
    rows, width = x_ref.shape
    padded[8:, :] = x_ref[...].astype(F32)
    padded[5:8, :] = rim_ref[...].astype(F32)
    total = jnp.zeros((rows, width), F32)
    for tap in range(4):
        total = total + weight_ref[tap : tap + 1, :] * padded[5 + tap : 5 + tap + rows, :]
    conv = silu(total)
    conv_ref[...] = conv
    part = lax.dot_general(
        proj_ref[...], conv.astype(BF16), (((0,), (1,)), ((), ())), preferred_element_type=F32
    )
    for index in range(8):
        part_ref[index] = part
    step = softplus(raw_ref[...].astype(F32) + bias_ref[...])
    drive = step * conv
    rate = -jnp.exp(decay_ref[...]) * LOG2E
    for index in range(width // 128):
        lanes = slice(index * 128, index * 128 + 128)
        step_ref[pl.ds(index, rows, stride=8), :] = step[:, lanes]
        drive_ref[pl.ds(index, rows, stride=8), :] = drive[:, lanes]
        rate_ref[pl.ds(index, rate.shape[0], stride=8), :] = rate[:, lanes]


def pack_state(states, total):
    high = total.astype(BF16).astype(F32)
    middle = (total - high).astype(BF16).astype(F32)
    low = total - high - middle
    tail = jnp.concatenate([high, middle, low, jnp.zeros_like(total)], axis=0)
    return jnp.concatenate(list(states) + [tail], axis=0).astype(BF16)


def unpack_state(ref, position):
    block = ref[position].astype(F32)
    states = [block[n * 8 : n * 8 + 8] for n in range(16)]
    return states, block[128:136] + block[136:144] + block[144:152]


def scan_kernel(coef_ref, step_ref, drive_ref, rate_ref, y_ref, sum_ref, end_ref):
    rows = step_ref.shape[0] // 8
    rates = [rate_ref[n * 8 : n * 8 + 8, :] for n in range(16)]
    zero = jnp.zeros((8, 128), F32)

    def advance(token, carry):
        total, states = carry
        here = pl.ds(pl.multiple_of(token * 8, 8), 8)
        step, drive = step_ref[here, :], drive_ref[here, :]
        total = total + step
        sum_ref[here, :] = total
        parts, following = [zero, zero], []
        for n in range(16):
            state = jnp.exp2(rates[n] * step) * states[n] + coef_ref[n, token] * drive
            parts[n % 2] = parts[n % 2] + coef_ref[16 + n, token] * state
            following.append(state)
        y_ref[here, :] = parts[0] + parts[1]
        return total, tuple(following)

    total, states = lax.fori_loop(0, rows, advance, (zero, (zero,) * 16), unroll=4)
    packed = pack_state(states, total)
    for index in range(8):
        end_ref[index] = packed


def fold(ref, rates, limit, states, total):
    for position in range(8):
        more, step = unpack_state(ref, position)
        keep = position < limit
        states = [
            jnp.where(keep, jnp.exp2(rates[n] * step) * states[n] + more[n], states[n])
            for n in range(16)
        ]
        total = jnp.where(keep, total + step, total)
    return states, total


def group_kernel(mine_ref, got_ref, rate_ref, before_ref, step_ref, all_ref):
    rates = [rate_ref[n * 8 : n * 8 + 8, :] for n in range(16)]
    zero = jnp.zeros((8, 128), F32)
    states, total = fold(got_ref, rates, mine_ref[0], [zero] * 16, zero)
    for n in range(16):
        before_ref[n * 8 : n * 8 + 8, :] = states[n]
    step_ref[...] = total
    states, total = fold(got_ref, rates, 8, [zero] * 16, zero)
    packed = pack_state(states, total)
    for index in range(8):
        all_ref[index] = packed


def finish_kernel(
    mine_ref,
    coef_ref,
    got_ref,
    rate_ref,
    before_ref,
    before_step_ref,
    y_ref,
    sum_ref,
    conv_ref,
    gain_ref,
    z_ref,
    out_ref,
    dense,
):
    rows, width = conv_ref.shape
    rates = [rate_ref[n * 8 : n * 8 + 8, :] for n in range(16)]
    zero = jnp.zeros((8, 128), F32)
    states, _ = fold(got_ref, rates, mine_ref[0], [zero] * 16, zero)
    states = [
        jnp.exp2(rates[n] * before_step_ref[...]) * states[n] + before_ref[n * 8 : n * 8 + 8, :]
        for n in range(16)
    ]

    def advance(token, carry):
        here = pl.ds(pl.multiple_of(token * 8, 8), 8)
        total = sum_ref[here, :]
        parts = [y_ref[here, :], zero]
        for n in range(16):
            parts[n % 2] = parts[n % 2] + coef_ref[16 + n, token] * (
                jnp.exp2(rates[n] * total) * states[n]
            )
        dense[here, :] = parts[0] + parts[1]
        return carry

    lax.fori_loop(0, rows, advance, 0, unroll=4)
    for index in range(width // 128):
        lanes = slice(index * 128, index * 128 + 128)
        value = dense[pl.ds(index, rows, stride=8), :]
        value = value + gain_ref[:, lanes] * conv_ref[:, lanes]
        out_ref[:, lanes] = (value * silu(z_ref[:, lanes].astype(F32))).astype(BF16)


def shards(
    inner_x,
    inner_z,
    step_raw,
    conv_weight,
    state_proj,
    step_bias,
    decay_log,
    skip_gain,
    moe_tokens,
    routes,
    gate_weight,
    up_weight,
):
    rows, width = inner_x.shape
    shards_of = lax.axis_size(SEQ)
    rim = lax.ppermute(inner_x[rows - 3 :], SEQ, [(i, i + 1) for i in range(shards_of - 1)])
    swap = [(0, 1), (1, 0)]
    features = moe_tokens.shape[1]
    placed = call(
        place_kernel, shape((8, CAP, features), BF16), [WHOLE] * 2, name="place", flops=1 << 28
    )(routes, moe_tokens)
    arrived = lax.all_to_all(placed, "exp", split_axis=0, concat_axis=0, tiled=True)
    weight = jnp.concatenate([gate_weight[0], up_weight[0]], axis=0)
    weights = [weight, lax.ppermute(weight, "c", swap)]

    dense = shape((rows * width // 128, 128), F32)
    conv, step, drive, rate, part = call(
        conv_kernel,
        (
            shape((rows, width), F32),
            dense,
            dense,
            shape((128, 128), F32),
            shape((8, 32, rows), F32),
        ),
        [WHOLE] * 7,
        [pltpu.VMEM((rows + 8, width), F32)],
        name="conv", flops=1 << 29,
    )(inner_x, rim, step_raw, conv_weight, state_proj, step_bias[None], decay_log)
    arrived, _, _ = lax.optimization_barrier((arrived, part, weight))
    first, rest = call(
        unpack_kernel,
        (shape((FIRST, 4096), BF16), shape((8, REST, 4096), BF16)),
        [WHOLE],
        [pltpu.VMEM((CAP, 4096), F32)],
        name="unpack",
        vmem=16,
        flops=1 << 28,
    )(arrived)
    shifted = [
        lax.ppermute(first, "x", [(i, (i + step) % 4) for i in range(4)]) for step in (1, 3, 2)
    ]
    first = call(
        join_kernel,
        shape((4 * FIRST, 4096), BF16),
        [WHOLE] * 4,
        [pltpu.VMEM((4 * FIRST, 4096), F32)],
        name="join",
        flops=1 << 28,
    )(first, *shifted)
    first = lax.all_gather(first, "z", axis=0, tiled=True)
    coef = jnp.sum(lax.all_to_all(part, "exp", split_axis=0, concat_axis=0, tiled=True), axis=0)
    rest, coef = lax.optimization_barrier((rest, coef))
    rest = lax.all_to_all(rest, "z", split_axis=0, concat_axis=0, tiled=True).reshape(-1, 4096)
    half = rest.shape[0] // 2
    ahead, back = ([(i, (i + step) % 4) for i in range(4)] for step in (1, 3))
    left, right = lax.ppermute(rest, "x", ahead), lax.ppermute(rest, "x", back)
    far_left = lax.ppermute(left[:half], "x", ahead)
    far_right = lax.ppermute(right[half:], "x", back)
    packed = shape((8, 160, 128), BF16)
    local, sums, ends = call(
        scan_kernel, (dense, dense, packed), [SMEM] + [WHOLE] * 3, name="scan", flops=1 << 31
    )(coef, step, drive, rate)
    ends, _ = lax.optimization_barrier((ends, rest))
    near = lax.all_to_all(ends, ("x", "c"), split_axis=0, concat_axis=0, tiled=True)
    place_in = lax.axis_index(("x", "c")).astype(jnp.int32).reshape(1)
    before, before_step, whole = call(
        group_kernel,
        (shape((128, 128), F32), shape((8, 128), F32), packed),
        [SMEM, WHOLE, WHOLE],
        name="group", vmem=16, flops=1 << 28,
    )(place_in, near, rate)
    far = lax.all_to_all(whole, "z", split_axis=0, concat_axis=0, tiled=True)
    layer = lax.axis_index("z").astype(jnp.int32).reshape(1)
    mixed = call(
        finish_kernel,
        shape((rows, width), BF16),
        [SMEM, SMEM] + [WHOLE] * 9,
        [pltpu.VMEM(dense.shape, F32)],
        name="finish", flops=1 << 31,
    )(layer, coef, far, rate, before, before_step, local, sums, conv, skip_gain[None], inner_z)

    theirs_rest, mine_rest = expand(weights, [rest, left, right, far_left, far_right], "expand_rest")
    theirs, mine = expand(weights, [first], "expand_first")
    other_rest = lax.ppermute(theirs_rest, "c", swap)
    other = lax.ppermute(theirs, "c", swap)
    here = [lax.axis_index(axis).astype(jnp.int32).reshape(1) for axis in ("x", "c")]
    units = gate_weight.shape[1]
    hidden = call(
        order_kernel,
        shape((units, 1280), BF16),
        [SMEM] * 2 + [WHOLE] * 4,
        name="order",
        flops=1 << 28,
    )(*here, mine, mine_rest, other, other_rest)[None]
    return mixed, hidden


def solution(mesh):
    fine = Mesh(mesh.devices.reshape(8, 4, 2, 8), ("z", "x", "c", "exp"))
    return jax.shard_map(
        shards,
        mesh=fine,
        in_specs=(
            P(SEQ, "exp"),
            P(SEQ, "exp"),
            P(SEQ, "exp"),
            P(None, "exp"),
            P("exp", None),
            P("exp"),
            P(None, "exp"),
            P("exp"),
            P(SEQ, "exp"),
            P(SEQ, None),
            P("exp", SEQ, None),
            P("exp", SEQ, None),
        ),
        out_specs=(P(SEQ, "exp"), P("exp", SEQ, None)),
        check_vma=False,
    )
```

```python
import jax
import jax.numpy as jnp
from jax import lax
from jax.experimental import pallas as pl
from jax.experimental.pallas import tpu as pltpu
from jax.sharding import Mesh
from jax.sharding import PartitionSpec as P

CAP = 20
F32 = jnp.float32
BF16 = jnp.bfloat16
LOG2E = 1.4426950408889634
SEQ = ("z", "x", "c")

VMEM = pl.BlockSpec(memory_space=pltpu.VMEM)
SMEM = pl.BlockSpec(memory_space=pltpu.SMEM)
WHOLE = pl.BlockSpec(memory_space=pltpu.HBM)


def call(kernel, out_shape, in_specs, scratch=(), name=None, vmem=60, flops=0):
    single = not isinstance(out_shape, tuple)
    outs = (out_shape,) if single else out_shape

    def run(*operands):
        moved = [index for index in range(len(in_specs)) if in_specs[index] is WHOLE]
        buffers = [pltpu.VMEM(operands[index].shape, operands[index].dtype) for index in moved]
        buffers += [pltpu.VMEM(out.shape, out.dtype) for out in outs]
        count = len(operands)

        def body(*refs):
            inputs, results = list(refs[:count]), refs[count : count + len(outs)]
            held = refs[count + len(outs) : count + len(outs) + len(buffers)]
            rest, sems = refs[count + len(outs) + len(buffers) : -1], refs[-1]
            copies = []
            for place, index in enumerate(moved):
                copies.append(pltpu.make_async_copy(inputs[index], held[place], sems.at[place]))
                inputs[index] = held[place]
            for copy in copies:
                copy.start()
            for copy in copies:
                copy.wait()
            made = held[len(moved) :]
            kernel(*inputs, *made, *rest)
            copies = [
                pltpu.make_async_copy(source, target, sems.at[len(moved) + place])
                for place, (source, target) in enumerate(zip(made, results))
            ]
            for copy in copies:
                copy.start()
            for copy in copies:
                copy.wait()

        found = pl.pallas_call(
            body,
            out_shape=outs,
            in_specs=in_specs,
            out_specs=(WHOLE,) * len(outs),
            scratch_shapes=[*buffers, *scratch, pltpu.SemaphoreType.DMA((len(buffers),))],
            name=name,
            compiler_params=pltpu.CompilerParams(vmem_limit_bytes=vmem << 20),
            cost_estimate=pl.CostEstimate(flops=flops, transcendentals=0, bytes_accessed=4 << 20),
        )(*operands)
        return found[0] if single else found

    return run


def shape(dims, dtype):
    return jax.ShapeDtypeStruct(dims, dtype)


def place_kernel(routes_ref, tokens_ref, out_ref, wide):
    rows = tokens_ref.shape[0]
    column = lax.broadcasted_iota(jnp.int32, (rows, 256), 1)
    expert, slot = column >> 5, column & 31
    named = (routes_ref[:, 0:1] == expert) | (routes_ref[:, 1:2] == expert)
    earlier = lax.broadcasted_iota(jnp.int32, (rows, rows), 0) > lax.broadcasted_iota(
        jnp.int32, (rows, rows), 1
    )
    before = jnp.dot(
        jnp.where(earlier, 1.0, 0.0).astype(BF16),
        jnp.where(named, 1.0, 0.0).astype(BF16),
        preferred_element_type=F32,
    )
    table = jnp.where(named & (before == slot.astype(F32)), 1.0, 0.0).astype(BF16)
    placed = lax.dot_general(
        table, tokens_ref[...], (((0,), (0,)), ((), ())), preferred_element_type=F32
    )
    for index in range(8):
        rows = placed[index * 32 : index * 32 + CAP]
        wide[:CAP, :], wide[CAP:, :] = rows[:, :256], rows[:, 256:]
        packed = wide[...].astype(BF16)
        for copy in range(4):
            out_ref[index * 4 + copy] = packed


def assemble_kernel(got_ref, out_ref, wide):
    for index in range(32):
        rows = got_ref[index].astype(F32)
        here = pl.ds(index % 4 * CAP, CAP)
        start = index // 4 * 512
        wide[here, start : start + 256] = rows[:CAP]
        wide[here, start + 256 : start + 512] = rows[CAP:]
    out_ref[...] = wide[...].astype(BF16)


def expand_kernel(rows_ref, weight_ref, out_ref, rows, weight, hidden, sems):
    count = rows.shape[0]
    chunks = [(start, min(256, count - start)) for start in range(0, count, 256)]
    copies = [pltpu.make_async_copy(weight_ref, weight, sems.at[0])]
    for index, (start, size) in enumerate(chunks):
        part = pl.ds(start, size)
        copies.append(pltpu.make_async_copy(rows_ref.at[part], rows.at[part], sems.at[1 + index]))
    for copy in copies:
        copy.start()
    copies[0].wait()
    units = hidden.shape[0]
    for copy, (start, size) in zip(copies[1:], chunks):
        copy.wait()
        both = lax.dot_general(
            weight[...],
            rows[start : start + size, :],
            (((1,), (1,)), ((), ())),
            preferred_element_type=F32,
        )
        hidden[:, start : start + size] = (silu(both[:units]) * both[units:]).astype(BF16)
    copy = pltpu.make_async_copy(hidden, out_ref, sems.at[0])
    copy.start()
    copy.wait()


def expand(rows, weight, name):
    units, count = weight.shape[0] // 2, rows.shape[0]
    out = shape((units, count), BF16)
    return pl.pallas_call(
        expand_kernel,
        out_shape=out,
        in_specs=[WHOLE] * 2,
        out_specs=WHOLE,
        scratch_shapes=[
            pltpu.VMEM(rows.shape, BF16),
            pltpu.VMEM(weight.shape, BF16),
            pltpu.VMEM(out.shape, BF16),
            pltpu.SemaphoreType.DMA((1 + pl.cdiv(count, 256),)),
        ],
        name=name,
        compiler_params=pltpu.CompilerParams(vmem_limit_bytes=60 << 20),
        cost_estimate=pl.CostEstimate(
            flops=4 * units * count * 4096, transcendentals=0, bytes_accessed=8 << 20
        ),
    )(rows, weight)


def divided(value, by):
    return (value * (65536 // by + 1)) >> 16


def order_kernel(core_ref, mine_ref, other_ref, out_ref):
    columns = out_ref.shape[1]
    count = mine_ref.shape[1]
    row = lax.broadcasted_iota(jnp.int32, (count, 1), 0)
    block = divided(row, CAP)
    base = row + (block + core_ref[0]) * CAP
    column = lax.broadcasted_iota(jnp.int32, (count, columns), 1)
    total = jnp.zeros(out_ref.shape, F32)
    for ref, target in ((mine_ref, base), (other_ref, base + (1 - 2 * core_ref[0]) * CAP)):
        table = jnp.where(column == target, 1.0, 0.0).astype(BF16)
        total = total + jnp.dot(ref[...], table, preferred_element_type=F32)
    out_ref[...] = total.astype(BF16)


def silu(value):
    return value / (1.0 + jnp.exp(-value))


def softplus(value):
    small = jnp.exp(-jnp.abs(value))
    ratio = small / (2.0 + small)
    square = ratio * ratio
    series = jnp.full_like(square, 1.0 / 15.0)
    for odd in (13, 11, 9, 7, 5, 3):
        series = series * square + 1.0 / odd
    return jnp.maximum(value, 0.0) + 2.0 * ratio * (series * square + 1.0)


def conv_kernel(
    x_ref,
    rim_ref,
    raw_ref,
    weight_ref,
    proj_ref,
    bias_ref,
    decay_ref,
    conv_ref,
    step_ref,
    drive_ref,
    rate_ref,
    part_ref,
    padded,
):
    rows, width = x_ref.shape
    padded[8:, :] = x_ref[...].astype(F32)
    padded[5:8, :] = rim_ref[...].astype(F32)
    total = jnp.zeros((rows, width), F32)
    for tap in range(4):
        total = total + weight_ref[tap : tap + 1, :] * padded[5 + tap : 5 + tap + rows, :]
    conv = silu(total)
    conv_ref[...] = conv
    part = lax.dot_general(
        proj_ref[...], conv.astype(BF16), (((0,), (1,)), ((), ())), preferred_element_type=F32
    )
    for index in range(8):
        part_ref[index] = part
    step = softplus(raw_ref[...].astype(F32) + bias_ref[...])
    drive = step * conv
    rate = -jnp.exp(decay_ref[...]) * LOG2E
    for index in range(width // 128):
        lanes = slice(index * 128, index * 128 + 128)
        step_ref[pl.ds(index, rows, stride=8), :] = step[:, lanes]
        drive_ref[pl.ds(index, rows, stride=8), :] = drive[:, lanes]
        rate_ref[pl.ds(index, rate.shape[0], stride=8), :] = rate[:, lanes]


def pack_state(states, total):
    high = total.astype(BF16).astype(F32)
    middle = (total - high).astype(BF16).astype(F32)
    low = total - high - middle
    tail = jnp.concatenate([high, middle, low, jnp.zeros_like(total)], axis=0)
    return jnp.concatenate(list(states) + [tail], axis=0).astype(BF16)


def unpack_state(ref, position):
    block = ref[position].astype(F32)
    states = [block[n * 8 : n * 8 + 8] for n in range(16)]
    return states, block[128:136] + block[136:144] + block[144:152]


def scan_kernel(coef_ref, step_ref, drive_ref, rate_ref, y_ref, sum_ref, end_ref):
    rows = step_ref.shape[0] // 8
    rates = [rate_ref[n * 8 : n * 8 + 8, :] for n in range(16)]
    zero = jnp.zeros((8, 128), F32)

    def advance(token, carry):
        total, states = carry
        here = pl.ds(pl.multiple_of(token * 8, 8), 8)
        step, drive = step_ref[here, :], drive_ref[here, :]
        total = total + step
        sum_ref[here, :] = total
        parts, following = [zero, zero], []
        for n in range(16):
            state = jnp.exp2(rates[n] * step) * states[n] + coef_ref[n, token] * drive
            parts[n % 2] = parts[n % 2] + coef_ref[16 + n, token] * state
            following.append(state)
        y_ref[here, :] = parts[0] + parts[1]
        return total, tuple(following)

    total, states = lax.fori_loop(0, rows, advance, (zero, (zero,) * 16), unroll=4)
    packed = pack_state(states, total)
    for index in range(8):
        end_ref[index] = packed


def fold(ref, rates, limit, states, total):
    for position in range(8):
        more, step = unpack_state(ref, position)
        keep = position < limit
        states = [
            jnp.where(keep, jnp.exp2(rates[n] * step) * states[n] + more[n], states[n])
            for n in range(16)
        ]
        total = jnp.where(keep, total + step, total)
    return states, total


def group_kernel(mine_ref, got_ref, rate_ref, before_ref, step_ref, all_ref):
    rates = [rate_ref[n * 8 : n * 8 + 8, :] for n in range(16)]
    zero = jnp.zeros((8, 128), F32)
    states, total = fold(got_ref, rates, mine_ref[0], [zero] * 16, zero)
    for n in range(16):
        before_ref[n * 8 : n * 8 + 8, :] = states[n]
    step_ref[...] = total
    states, total = fold(got_ref, rates, 8, [zero] * 16, zero)
    packed = pack_state(states, total)
    for index in range(8):
        all_ref[index] = packed


def finish_kernel(
    mine_ref,
    coef_ref,
    got_ref,
    rate_ref,
    before_ref,
    before_step_ref,
    y_ref,
    sum_ref,
    conv_ref,
    gain_ref,
    z_ref,
    out_ref,
    dense,
):
    rows, width = conv_ref.shape
    rates = [rate_ref[n * 8 : n * 8 + 8, :] for n in range(16)]
    zero = jnp.zeros((8, 128), F32)
    states, _ = fold(got_ref, rates, mine_ref[0], [zero] * 16, zero)
    states = [
        jnp.exp2(rates[n] * before_step_ref[...]) * states[n] + before_ref[n * 8 : n * 8 + 8, :]
        for n in range(16)
    ]

    def advance(token, carry):
        here = pl.ds(pl.multiple_of(token * 8, 8), 8)
        total = sum_ref[here, :]
        parts = [y_ref[here, :], zero]
        for n in range(16):
            parts[n % 2] = parts[n % 2] + coef_ref[16 + n, token] * (
                jnp.exp2(rates[n] * total) * states[n]
            )
        dense[here, :] = parts[0] + parts[1]
        return carry

    lax.fori_loop(0, rows, advance, 0, unroll=4)
    for index in range(width // 128):
        lanes = slice(index * 128, index * 128 + 128)
        value = dense[pl.ds(index, rows, stride=8), :]
        value = value + gain_ref[:, lanes] * conv_ref[:, lanes]
        out_ref[:, lanes] = (value * silu(z_ref[:, lanes].astype(F32))).astype(BF16)


def shards(
    inner_x,
    inner_z,
    step_raw,
    conv_weight,
    state_proj,
    step_bias,
    decay_log,
    skip_gain,
    moe_tokens,
    routes,
    gate_weight,
    up_weight,
):
    rows, width = inner_x.shape
    shards_of = lax.axis_size(SEQ)
    rim = lax.ppermute(inner_x[rows - 3 :], SEQ, [(i, i + 1) for i in range(shards_of - 1)])
    swap = [(0, 1), (1, 0)]
    features = moe_tokens.shape[1]
    placed = call(
        place_kernel,
        shape((32, 2 * CAP, features // 2), BF16),
        [WHOLE] * 2,
        [pltpu.VMEM((2 * CAP, features // 2), F32)],
        name="place",
        flops=1 << 28,
    )(routes, moe_tokens)
    arrived = lax.all_to_all(placed, ("exp", "x"), split_axis=0, concat_axis=0, tiled=True)
    weight = jnp.concatenate([gate_weight[0], up_weight[0]], axis=0)
    other_weight = lax.ppermute(weight, "c", swap)

    dense = shape((rows * width // 128, 128), F32)
    conv, step, drive, rate, part = call(
        conv_kernel,
        (
            shape((rows, width), F32),
            dense,
            dense,
            shape((128, 128), F32),
            shape((8, 32, rows), F32),
        ),
        [WHOLE] * 7,
        [pltpu.VMEM((rows + 8, width), F32)],
        name="conv", flops=1 << 29,
    )(inner_x, rim, step_raw, conv_weight, state_proj, step_bias[None], decay_log)
    arrived, _, _ = lax.optimization_barrier((arrived, part, weight))
    block = call(
        assemble_kernel,
        shape((4 * CAP, 4096), BF16),
        [WHOLE],
        [pltpu.VMEM((4 * CAP, 4096), F32)],
        name="assemble",
        vmem=16,
        flops=1 << 28,
    )(arrived)
    gathered = lax.all_gather(block, "z", axis=0, tiled=True)
    coef = jnp.sum(lax.all_to_all(part, "exp", split_axis=0, concat_axis=0, tiled=True), axis=0)
    packed = shape((8, 160, 128), BF16)
    local, sums, ends = call(
        scan_kernel, (dense, dense, packed), [SMEM] + [WHOLE] * 3, name="scan", flops=1 << 31
    )(coef, step, drive, rate)
    near = lax.all_to_all(ends, ("x", "c"), split_axis=0, concat_axis=0, tiled=True)
    place_in = lax.axis_index(("x", "c")).astype(jnp.int32).reshape(1)
    before, before_step, whole = call(
        group_kernel,
        (shape((128, 128), F32), shape((8, 128), F32), packed),
        [SMEM, WHOLE, WHOLE],
        name="group", vmem=16, flops=1 << 28,
    )(place_in, near, rate)
    far = lax.all_to_all(whole, "z", split_axis=0, concat_axis=0, tiled=True)
    far, other_weight = lax.optimization_barrier((far, other_weight))
    layer = lax.axis_index("z").astype(jnp.int32).reshape(1)
    mixed = call(
        finish_kernel,
        shape((rows, width), BF16),
        [SMEM, SMEM] + [WHOLE] * 9,
        [pltpu.VMEM(dense.shape, F32)],
        name="finish", flops=1 << 31,
    )(layer, coef, far, rate, before, before_step, local, sums, conv, skip_gain[None], inner_z)

    gathered, mixed = lax.optimization_barrier((gathered, mixed))
    other = lax.ppermute(expand(gathered, other_weight, "expand_other"), "c", swap)
    mine = expand(gathered, weight, "expand_mine")
    core = lax.axis_index("c").astype(jnp.int32).reshape(1)
    hidden = call(
        order_kernel,
        shape((gate_weight.shape[1], 1280), BF16),
        [SMEM, WHOLE, WHOLE],
        name="order",
        flops=1 << 28,
    )(core, mine, other)[None]
    return mixed, hidden


def solution(mesh):
    fine = Mesh(mesh.devices.reshape(8, 4, 2, 8), ("z", "x", "c", "exp"))
    return jax.shard_map(
        shards,
        mesh=fine,
        in_specs=(
            P(SEQ, "exp"),
            P(SEQ, "exp"),
            P(SEQ, "exp"),
            P(None, "exp"),
            P("exp", None),
            P("exp"),
            P(None, "exp"),
            P("exp"),
            P(SEQ, "exp"),
            P(SEQ, None),
            P("exp", SEQ, None),
            P("exp", SEQ, None),
        ),
        out_specs=(P(SEQ, "exp"), P("exp", SEQ, None)),
        check_vma=False,
    )
```

```python
import functools

import jax
import jax.numpy as jnp
from jax import lax
from jax.experimental import pallas as pl
from jax.experimental.pallas import tpu as pltpu
from jax.sharding import Mesh
from jax.sharding import PartitionSpec as P

CAP = 20
F32 = jnp.float32
BF16 = jnp.bfloat16
LOG2E = 1.4426950408889634
SEQ = ("z", "x", "c")

VMEM = pl.BlockSpec(memory_space=pltpu.VMEM)
SMEM = pl.BlockSpec(memory_space=pltpu.SMEM)
WHOLE = pl.BlockSpec(memory_space=pltpu.HBM)


def call(kernel, out_shape, in_specs, scratch=(), name=None, vmem=60, flops=0):
    single = not isinstance(out_shape, tuple)
    outs = (out_shape,) if single else out_shape

    def run(*operands):
        moved = [index for index in range(len(in_specs)) if in_specs[index] is WHOLE]
        buffers = [pltpu.VMEM(operands[index].shape, operands[index].dtype) for index in moved]
        buffers += [pltpu.VMEM(out.shape, out.dtype) for out in outs]
        count = len(operands)

        def body(*refs):
            inputs, results = list(refs[:count]), refs[count : count + len(outs)]
            held = refs[count + len(outs) : count + len(outs) + len(buffers)]
            rest, sems = refs[count + len(outs) + len(buffers) : -1], refs[-1]
            copies = []
            for place, index in enumerate(moved):
                copies.append(pltpu.make_async_copy(inputs[index], held[place], sems.at[place]))
                inputs[index] = held[place]
            for copy in copies:
                copy.start()
            for copy in copies:
                copy.wait()
            made = held[len(moved) :]
            kernel(*inputs, *made, *rest)
            copies = [
                pltpu.make_async_copy(source, target, sems.at[len(moved) + place])
                for place, (source, target) in enumerate(zip(made, results))
            ]
            for copy in copies:
                copy.start()
            for copy in copies:
                copy.wait()

        found = pl.pallas_call(
            body,
            out_shape=outs,
            in_specs=in_specs,
            out_specs=(WHOLE,) * len(outs),
            scratch_shapes=[*buffers, *scratch, pltpu.SemaphoreType.DMA((len(buffers),))],
            name=name,
            compiler_params=pltpu.CompilerParams(vmem_limit_bytes=vmem << 20),
            cost_estimate=pl.CostEstimate(flops=flops, transcendentals=0, bytes_accessed=4 << 20),
        )(*operands)
        return found[0] if single else found

    return run


def shape(dims, dtype):
    return jax.ShapeDtypeStruct(dims, dtype)


def place_kernel(routes_ref, tokens_ref, out_ref, wide):
    tokens = tokens_ref.shape[0]
    row = lax.broadcasted_iota(jnp.int32, (256, tokens), 0)
    expert, slot = row >> 5, row & 31
    named = (routes_ref[0:1, :] == expert) | (routes_ref[1:2, :] == expert)
    earlier = lax.broadcasted_iota(jnp.int32, (tokens, tokens), 0) < lax.broadcasted_iota(
        jnp.int32, (tokens, tokens), 1
    )
    before = jnp.dot(
        jnp.where(named, 1.0, 0.0).astype(BF16),
        jnp.where(earlier, 1.0, 0.0).astype(BF16),
        preferred_element_type=F32,
    )
    table = jnp.where(named & (before == slot.astype(F32)), 1.0, 0.0).astype(BF16)
    placed = jnp.dot(table, tokens_ref[...], preferred_element_type=F32)
    for index in range(8):
        rows = placed[index * 32 : index * 32 + CAP]
        wide[:CAP, :], wide[CAP:, :] = rows[:, :256], rows[:, 256:]
        packed = wide[...].astype(BF16)
        for copy in range(4):
            out_ref[index * 4 + copy] = packed


def assemble_kernel(got_ref, out_ref, wide):
    for index in range(32):
        rows = got_ref[index].astype(F32)
        here = pl.ds(index % 4 * CAP, CAP)
        start = index // 4 * 512
        wide[here, start : start + 256] = rows[:CAP]
        wide[here, start + 256 : start + 512] = rows[CAP:]
    out_ref[...] = wide[...].astype(BF16)


def expand_kernel(blocks, pairs, *refs):
    inputs = blocks + 2 * pairs
    sources, outs, refs = refs[:inputs], refs[inputs : inputs + pairs], refs[inputs + pairs :]
    rows, held, made, sems = refs[0], refs[1 : 1 + pairs], refs[1 + pairs : -1], refs[-1]
    copies, start = [], 0
    for source in sources[:blocks]:
        size = source.shape[0]
        copies.append((source, rows.at[pl.ds(start, size)]))
        start += size
    units = made[0].shape[0]
    for index, source in enumerate(sources[blocks:]):
        target = held[index // 2].at[pl.ds(index % 2 * units, units)]
        copies.append((source, target))
    copies = [
        pltpu.make_async_copy(source, target, sems.at[index])
        for index, (source, target) in enumerate(copies)
    ]
    for copy in copies[blocks:] + copies[:blocks]:
        copy.start()
    for copy in copies[:blocks]:
        copy.wait()
    sent = []
    for index, (weight, hidden, out) in enumerate(zip(held, made, outs)):
        for copy in copies[blocks + 2 * index : blocks + 2 * index + 2]:
            copy.wait()
        both = lax.dot_general(
            weight[...], rows[...], (((1,), (1,)), ((), ())), preferred_element_type=F32
        )
        hidden[...] = (silu(both[:units]) * both[units:]).astype(BF16)
        sent.append(pltpu.make_async_copy(hidden, out, sems.at[inputs + index]))
        sent[-1].start()
    for copy in sent:
        copy.wait()


def expand(blocks, pairs, name):
    weights = [weight for pair in pairs for weight in pair]
    units, count = weights[0].shape[0], sum(block.shape[0] for block in blocks)
    out = shape((units, count), BF16)
    total = len(pairs)
    return pl.pallas_call(
        functools.partial(expand_kernel, len(blocks), total),
        out_shape=(out,) * total,
        in_specs=[WHOLE] * (len(blocks) + 2 * total),
        out_specs=(WHOLE,) * total,
        scratch_shapes=[
            pltpu.VMEM((count, 4096), BF16),
            *[pltpu.VMEM((2 * units, 4096), BF16)] * total,
            *[pltpu.VMEM(out.shape, BF16)] * total,
            pltpu.SemaphoreType.DMA((len(blocks) + 3 * total,)),
        ],
        name=name,
        compiler_params=pltpu.CompilerParams(vmem_limit_bytes=60 << 20),
        cost_estimate=pl.CostEstimate(
            flops=4 * total * units * count * 4096, transcendentals=0, bytes_accessed=8 << 20
        ),
    )(*blocks, *weights)


def divided(value, by):
    return (value * (65536 // by + 1)) >> 16


EARLY = ((0, 0), (1, 0), (1, 1), (2, 0), (2, 1))
LATE = ((3, 0), (3, 1), (4, 0))


def order_kernel(place_ref, mine_early, mine_late, other_early, other_late, out_ref):
    columns = out_ref.shape[1]
    total = jnp.zeros(out_ref.shape, F32)
    for pair, blocks in (((mine_early, other_early), EARLY), ((mine_late, other_late), LATE)):
        count = pair[0].shape[1]
        row = lax.broadcasted_iota(jnp.int32, (count, 1), 0)
        block = divided(row, 4 * CAP)
        within = row - block * (4 * CAP)
        steps, twin = (jnp.full_like(row, value) for value in blocks[0])
        for index, (step, other) in enumerate(blocks[1:], 1):
            steps = jnp.where(block == index, step, steps)
            twin = jnp.where(block == index, other, twin)
        base = within + divided(within, CAP) * CAP
        column = lax.broadcasted_iota(jnp.int32, (count, columns), 1)
        for ref, holder in zip(pair, (place_ref[1], 1 - place_ref[1])):
            layer = (place_ref[0] + steps * (2 * holder - 1)) & 7
            core = holder + twin * (1 - 2 * holder)
            target = layer * (8 * CAP) + core * CAP + base
            table = jnp.where(column == target, 1.0, 0.0).astype(BF16)
            total = total + jnp.dot(ref[...], table, preferred_element_type=F32)
    out_ref[...] = total.astype(BF16)


def silu(value):
    return value / (1.0 + jnp.exp(-value))


def softplus(value):
    small = jnp.exp(-jnp.abs(value))
    ratio = small / (2.0 + small)
    square = ratio * ratio
    series = jnp.full_like(square, 1.0 / 15.0)
    for odd in (13, 11, 9, 7, 5, 3):
        series = series * square + 1.0 / odd
    return jnp.maximum(value, 0.0) + 2.0 * ratio * (series * square + 1.0)


def conv_kernel(
    x_ref,
    rim_ref,
    raw_ref,
    weight_ref,
    proj_ref,
    bias_ref,
    decay_ref,
    conv_ref,
    step_ref,
    drive_ref,
    rate_ref,
    part_ref,
    padded,
):
    rows, width = x_ref.shape
    padded[8:, :] = x_ref[...].astype(F32)
    padded[5:8, :] = rim_ref[...].astype(F32)
    total = jnp.zeros((rows, width), F32)
    for tap in range(4):
        total = total + weight_ref[tap : tap + 1, :] * padded[5 + tap : 5 + tap + rows, :]
    conv = silu(total)
    conv_ref[...] = conv
    part = lax.dot_general(
        proj_ref[...], conv.astype(BF16), (((1,), (1,)), ((), ())), preferred_element_type=F32
    )
    for index in range(8):
        part_ref[index] = part
    step = softplus(raw_ref[...].astype(F32) + bias_ref[...])
    drive = step * conv
    rate = -jnp.exp(decay_ref[...]) * LOG2E
    for index in range(width // 128):
        lanes = slice(index * 128, index * 128 + 128)
        step_ref[pl.ds(index, rows, stride=8), :] = step[:, lanes]
        drive_ref[pl.ds(index, rows, stride=8), :] = drive[:, lanes]
        rate_ref[pl.ds(index, rate.shape[0], stride=8), :] = rate[:, lanes]


def pack_state(states, total):
    high = total.astype(BF16).astype(F32)
    middle = (total - high).astype(BF16).astype(F32)
    low = total - high - middle
    tail = jnp.concatenate([high, middle, low, jnp.zeros_like(total)], axis=0)
    return jnp.concatenate(list(states) + [tail], axis=0).astype(BF16)


def unpack_state(ref, position):
    block = ref[position].astype(F32)
    states = [block[n * 8 : n * 8 + 8] for n in range(16)]
    return states, block[128:136] + block[136:144] + block[144:152]


def scan_kernel(coef_ref, step_ref, drive_ref, rate_ref, y_ref, sum_ref, end_ref):
    rows = step_ref.shape[0] // 8
    rates = [rate_ref[n * 8 : n * 8 + 8, :] for n in range(16)]
    zero = jnp.zeros((8, 128), F32)

    def advance(token, carry):
        total, states = carry
        here = pl.ds(pl.multiple_of(token * 8, 8), 8)
        step, drive = step_ref[here, :], drive_ref[here, :]
        total = total + step
        sum_ref[here, :] = total
        parts, following = [zero, zero], []
        for n in range(16):
            state = jnp.exp2(rates[n] * step) * states[n] + coef_ref[n, token] * drive
            parts[n % 2] = parts[n % 2] + coef_ref[16 + n, token] * state
            following.append(state)
        y_ref[here, :] = parts[0] + parts[1]
        return total, tuple(following)

    total, states = lax.fori_loop(0, rows, advance, (zero, (zero,) * 16), unroll=4)
    packed = pack_state(states, total)
    for index in range(8):
        end_ref[index] = packed


def fold(ref, rates, limit, states, total):
    for position in range(8):
        more, step = unpack_state(ref, position)
        keep = position < limit
        states = [
            jnp.where(keep, jnp.exp2(rates[n] * step) * states[n] + more[n], states[n])
            for n in range(16)
        ]
        total = jnp.where(keep, total + step, total)
    return states, total


def group_kernel(mine_ref, got_ref, rate_ref, before_ref, step_ref, all_ref):
    rates = [rate_ref[n * 8 : n * 8 + 8, :] for n in range(16)]
    zero = jnp.zeros((8, 128), F32)
    states, total = fold(got_ref, rates, mine_ref[0], [zero] * 16, zero)
    for n in range(16):
        before_ref[n * 8 : n * 8 + 8, :] = states[n]
    step_ref[...] = total
    states, total = fold(got_ref, rates, 8, [zero] * 16, zero)
    packed = pack_state(states, total)
    for index in range(8):
        all_ref[index] = packed


def finish_kernel(
    mine_ref,
    coef_ref,
    got_ref,
    rate_ref,
    before_ref,
    before_step_ref,
    y_ref,
    sum_ref,
    conv_ref,
    gain_ref,
    z_ref,
    out_ref,
    dense,
):
    rows, width = conv_ref.shape
    rates = [rate_ref[n * 8 : n * 8 + 8, :] for n in range(16)]
    zero = jnp.zeros((8, 128), F32)
    states, _ = fold(got_ref, rates, mine_ref[0], [zero] * 16, zero)
    states = [
        jnp.exp2(rates[n] * before_step_ref[...]) * states[n] + before_ref[n * 8 : n * 8 + 8, :]
        for n in range(16)
    ]

    def advance(token, carry):
        here = pl.ds(pl.multiple_of(token * 8, 8), 8)
        total = sum_ref[here, :]
        parts = [y_ref[here, :], zero]
        for n in range(16):
            parts[n % 2] = parts[n % 2] + coef_ref[16 + n, token] * (
                jnp.exp2(rates[n] * total) * states[n]
            )
        dense[here, :] = parts[0] + parts[1]
        return carry

    lax.fori_loop(0, rows, advance, 0, unroll=4)
    for index in range(width // 128):
        lanes = slice(index * 128, index * 128 + 128)
        value = dense[pl.ds(index, rows, stride=8), :]
        value = value + gain_ref[:, lanes] * conv_ref[:, lanes]
        out_ref[:, lanes] = (value * silu(z_ref[:, lanes].astype(F32))).astype(BF16)


def shards(
    inner_x,
    inner_z,
    step_raw,
    conv_weight,
    state_proj,
    step_bias,
    decay_log,
    skip_gain,
    moe_tokens,
    routes,
    gate_weight,
    up_weight,
):
    rows, width = inner_x.shape
    shards_of = lax.axis_size(SEQ)
    rim = lax.ppermute(inner_x[rows - 3 :], SEQ, [(i, i + 1) for i in range(shards_of - 1)])
    swap = [(0, 1), (1, 0)]
    features = moe_tokens.shape[1]
    placed = call(
        place_kernel,
        shape((32, 2 * CAP, features // 2), BF16),
        [WHOLE] * 2,
        [pltpu.VMEM((2 * CAP, features // 2), F32)],
        name="place",
        flops=1 << 28,
    )(routes.T, moe_tokens)
    arrived = lax.all_to_all(placed, ("exp", "x"), split_axis=0, concat_axis=0, tiled=True)
    dense = shape((rows * width // 128, 128), F32)
    conv, step, drive, rate, part = call(
        conv_kernel,
        (
            shape((rows, width), F32),
            dense,
            dense,
            shape((128, 128), F32),
            shape((8, 32, rows), F32),
        ),
        [WHOLE] * 7,
        [pltpu.VMEM((rows + 8, width), F32)],
        name="conv", flops=1 << 29,
    )(inner_x, rim, step_raw, conv_weight, state_proj.T, step_bias[None], decay_log)
    dense = shape((rows * width // 128, 128), F32)
    conv, step, drive, rate, part = call(
        conv_kernel,
        (
            shape((rows, width), F32),
            dense,
            dense,
            shape((128, 128), F32),
            shape((8, 32, rows), F32),
        ),
        [WHOLE] * 7,
        [pltpu.VMEM((rows + 8, width), F32)],
        name="conv", flops=1 << 29,
    )(inner_x, rim, step_raw, conv_weight, state_proj.T, step_bias[None], decay_log)
    weight = jnp.concatenate([gate_weight[0], up_weight[0]], axis=0)
    arrived, part = lax.optimization_barrier((arrived, part))
    block = call(
        assemble_kernel,
        shape((4 * CAP, 4096), BF16),
        [WHOLE],
        [pltpu.VMEM((4 * CAP, 4096), F32)],
        name="assemble",
        vmem=16,
        flops=1 << 28,
    )(arrived)
    onward = [(2 * z + c, 2 * ((z + 1 - 2 * c) % 8) + c) for z in range(8) for c in range(2)]

    def step_on(rows):
        return lax.ppermute(rows, ("z", "c"), onward)

    own, twin = [block, step_on(block)], [lax.ppermute(block, "c", swap)]
    twin[0], part = lax.optimization_barrier((twin[0], part))
    twin.append(step_on(twin[0]))
    coef = lax.all_to_all(part, "exp", split_axis=0, concat_axis=0, tiled=True)
    own[1], coef = lax.optimization_barrier((own[1], coef))
    coef = jnp.sum(coef, axis=0)
    packed = shape((8, 160, 128), BF16)
    local, sums, ends = call(
        scan_kernel, (dense, dense, packed), [SMEM] + [WHOLE] * 3, name="scan", flops=1 << 31
    )(coef, step, drive, rate)
    for _ in range(2):
        own.append(step_on(own[-1]))
        twin.append(step_on(twin[-1]))
    own.append(step_on(own[-1]))
    near = lax.all_to_all(ends, ("x", "c"), split_axis=0, concat_axis=0, tiled=True)
    place_in = lax.axis_index(("x", "c")).astype(jnp.int32).reshape(1)
    before, before_step, whole = call(
        group_kernel,
        (shape((128, 128), F32), shape((8, 128), F32), packed),
        [SMEM, WHOLE, WHOLE],
        name="group", vmem=16, flops=1 << 28,
    )(place_in, near, rate)
    far = lax.all_to_all(whole, "z", split_axis=0, concat_axis=0, tiled=True)
    layer = lax.axis_index("z").astype(jnp.int32).reshape(1)
    mixed = call(
        finish_kernel,
        shape((rows, width), BF16),
        [SMEM, SMEM] + [WHOLE] * 9,
        [pltpu.VMEM(dense.shape, F32)],
        name="finish", flops=1 << 31,
    )(layer, coef, far, rate, before, before_step, local, sums, conv, skip_gain[None], inner_z)

    weights = gate_weight[0], up_weight[0]
    *sent, _ = lax.optimization_barrier((*weights, ends))
    pairs = [[lax.ppermute(weight, "c", swap) for weight in sent], weights]
    other_early, mine_early = expand([block, own[1], twin[1], own[2], twin[2]], pairs, "expand_early")
    late = [own[3], twin[3], own[4]]
    (other_late,) = expand(late, pairs[:1], "expand_other")
    (mine_late,) = expand(late, pairs[1:], "expand_mine")
    others = [lax.ppermute(part, "c", swap) for part in (other_early, other_late)]
    here = jnp.stack([lax.axis_index("z"), lax.axis_index("c")]).astype(jnp.int32)
    hidden = call(
        order_kernel,
        shape((gate_weight.shape[1], 1280), BF16),
        [SMEM] + [WHOLE] * 4,
        name="order",
        flops=1 << 28,
    )(here, mine_early, mine_late, *others)[None]
    return mixed, hidden


def solution(mesh):
    fine = Mesh(mesh.devices.reshape(8, 4, 2, 8), ("z", "x", "c", "exp"))
    return jax.shard_map(
        shards,
        mesh=fine,
        in_specs=(
            P(SEQ, "exp"),
            P(SEQ, "exp"),
            P(SEQ, "exp"),
            P(None, "exp"),
            P("exp", None),
            P("exp"),
            P(None, "exp"),
            P("exp"),
            P(SEQ, "exp"),
            P(SEQ, None),
            P("exp", SEQ, None),
            P("exp", SEQ, None),
        ),
        out_specs=(P(SEQ, "exp"), P("exp", SEQ, None)),
        check_vma=False,
    )
```

```python
import functools

import jax
import jax.numpy as jnp
from jax import lax
from jax.experimental import pallas as pl
from jax.experimental.pallas import tpu as pltpu
from jax.sharding import Mesh
from jax.sharding import PartitionSpec as P

CAP = 20
F32 = jnp.float32
BF16 = jnp.bfloat16
LOG2E = 1.4426950408889634
SEQ = ("z", "x", "c")

VMEM = pl.BlockSpec(memory_space=pltpu.VMEM)
SMEM = pl.BlockSpec(memory_space=pltpu.SMEM)
WHOLE = pl.BlockSpec(memory_space=pltpu.HBM)


def call(kernel, out_shape, in_specs, scratch=(), name=None, vmem=60, flops=0):
    single = not isinstance(out_shape, tuple)
    outs = (out_shape,) if single else out_shape

    def run(*operands):
        moved = [index for index in range(len(in_specs)) if in_specs[index] is WHOLE]
        buffers = [pltpu.VMEM(operands[index].shape, operands[index].dtype) for index in moved]
        buffers += [pltpu.VMEM(out.shape, out.dtype) for out in outs]
        count = len(operands)

        def body(*refs):
            inputs, results = list(refs[:count]), refs[count : count + len(outs)]
            held = refs[count + len(outs) : count + len(outs) + len(buffers)]
            rest, sems = refs[count + len(outs) + len(buffers) : -1], refs[-1]
            copies = []
            for place, index in enumerate(moved):
                copies.append(pltpu.make_async_copy(inputs[index], held[place], sems.at[place]))
                inputs[index] = held[place]
            for copy in copies:
                copy.start()
            for copy in copies:
                copy.wait()
            made = held[len(moved) :]
            kernel(*inputs, *made, *rest)
            copies = [
                pltpu.make_async_copy(source, target, sems.at[len(moved) + place])
                for place, (source, target) in enumerate(zip(made, results))
            ]
            for copy in copies:
                copy.start()
            for copy in copies:
                copy.wait()

        found = pl.pallas_call(
            body,
            out_shape=outs,
            in_specs=in_specs,
            out_specs=(WHOLE,) * len(outs),
            scratch_shapes=[*buffers, *scratch, pltpu.SemaphoreType.DMA((len(buffers),))],
            name=name,
            compiler_params=pltpu.CompilerParams(vmem_limit_bytes=vmem << 20),
            cost_estimate=pl.CostEstimate(flops=flops, transcendentals=0, bytes_accessed=4 << 20),
        )(*operands)
        return found[0] if single else found

    return run


def shape(dims, dtype):
    return jax.ShapeDtypeStruct(dims, dtype)


def place_kernel(routes_ref, tokens_ref, out_ref, wide):
    tokens = tokens_ref.shape[0]
    row = lax.broadcasted_iota(jnp.int32, (256, tokens), 0)
    expert, slot = row >> 5, row & 31
    named = (routes_ref[0:1, :] == expert) | (routes_ref[1:2, :] == expert)
    earlier = lax.broadcasted_iota(jnp.int32, (tokens, tokens), 0) < lax.broadcasted_iota(
        jnp.int32, (tokens, tokens), 1
    )
    before = jnp.dot(
        jnp.where(named, 1.0, 0.0).astype(BF16),
        jnp.where(earlier, 1.0, 0.0).astype(BF16),
        preferred_element_type=F32,
    )
    table = jnp.where(named & (before == slot.astype(F32)), 1.0, 0.0).astype(BF16)
    placed = jnp.dot(table, tokens_ref[...], preferred_element_type=F32)
    for index in range(8):
        rows = placed[index * 32 : index * 32 + CAP]
        wide[:CAP, :], wide[CAP:, :] = rows[:, :256], rows[:, 256:]
        packed = wide[...].astype(BF16)
        for copy in range(4):
            out_ref[index * 4 + copy] = packed


def assemble_kernel(got_ref, out_ref, wide):
    for index in range(32):
        rows = got_ref[index].astype(F32)
        here = pl.ds(index % 4 * CAP, CAP)
        start = index // 4 * 512
        wide[here, start : start + 256] = rows[:CAP]
        wide[here, start + 256 : start + 512] = rows[CAP:]
    out_ref[...] = wide[...].astype(BF16)


def expand_kernel(blocks, pairs, *refs):
    inputs = blocks + 2 * pairs
    sources, outs, refs = refs[:inputs], refs[inputs : inputs + pairs], refs[inputs + pairs :]
    rows, held, made, sems = refs[0], refs[1 : 1 + pairs], refs[1 + pairs : -1], refs[-1]
    copies, start = [], 0
    for source in sources[:blocks]:
        size = source.shape[0]
        copies.append((source, rows.at[pl.ds(start, size)]))
        start += size
    units = made[0].shape[0]
    for index, source in enumerate(sources[blocks:]):
        target = held[index // 2].at[pl.ds(index % 2 * units, units)]
        copies.append((source, target))
    copies = [
        pltpu.make_async_copy(source, target, sems.at[index])
        for index, (source, target) in enumerate(copies)
    ]
    for copy in copies:
        copy.start()
    for copy in copies[:blocks]:
        copy.wait()
    sent = []
    for index, (weight, hidden, out) in enumerate(zip(held, made, outs)):
        for copy in copies[blocks + 2 * index : blocks + 2 * index + 2]:
            copy.wait()
        both = lax.dot_general(
            weight[...], rows[...], (((1,), (1,)), ((), ())), preferred_element_type=F32
        )
        hidden[...] = (silu(both[:units]) * both[units:]).astype(BF16)
        sent.append(pltpu.make_async_copy(hidden, out, sems.at[inputs + index]))
        sent[-1].start()
    for copy in sent:
        copy.wait()


def expand(blocks, pairs, name):
    weights = [weight for pair in pairs for weight in pair]
    units, count = weights[0].shape[0], sum(block.shape[0] for block in blocks)
    out = shape((units, count), BF16)
    total = len(pairs)
    return pl.pallas_call(
        functools.partial(expand_kernel, len(blocks), total),
        out_shape=(out,) * total,
        in_specs=[WHOLE] * (len(blocks) + 2 * total),
        out_specs=(WHOLE,) * total,
        scratch_shapes=[
            pltpu.VMEM((count, 4096), BF16),
            *[pltpu.VMEM((2 * units, 4096), BF16)] * total,
            *[pltpu.VMEM(out.shape, BF16)] * total,
            pltpu.SemaphoreType.DMA((len(blocks) + 3 * total,)),
        ],
        name=name,
        compiler_params=pltpu.CompilerParams(vmem_limit_bytes=60 << 20),
        cost_estimate=pl.CostEstimate(
            flops=4 * total * units * count * 4096, transcendentals=0, bytes_accessed=8 << 20
        ),
    )(*blocks, *weights)


def divided(value, by):
    return (value * (65536 // by + 1)) >> 16


EARLY = ((0, 0), (1, 0), (1, 1), (2, 0), (2, 1))
LATE = ((3, 0), (3, 1), (4, 0))


def last_kernel(place_ref, *refs):
    (*sources, out_ref), held = refs[:9], refs[9:-1]
    rows, weight, mine_early, other_early, other_late, mine_late, out, sems = *held, refs[-1]
    size, units = sources[0].shape[0], sources[3].shape[0]
    targets = [rows.at[pl.ds(index * size, size)] for index in range(3)]
    targets += [weight.at[pl.ds(index * units, units)] for index in range(2)]
    targets += [mine_early, other_early, other_late]
    copies = [
        pltpu.make_async_copy(source, target, sems.at[index])
        for index, (source, target) in enumerate(zip(sources, targets))
    ]
    for copy in copies:
        copy.start()
    for copy in copies:
        copy.wait()
    both = lax.dot_general(
        weight[...], rows[...], (((1,), (1,)), ((), ())), preferred_element_type=F32
    )
    mine_late[...] = (silu(both[:units]) * both[units:]).astype(BF16)
    places = []
    for pair, blocks in (((mine_early, other_early), EARLY), ((mine_late, other_late), LATE)):
        count = pair[0].shape[1]
        row = lax.broadcasted_iota(jnp.int32, (count, 1), 0)
        block = divided(row, 4 * CAP)
        within = row - block * (4 * CAP)
        steps, twin = (jnp.full_like(row, value) for value in blocks[0])
        for index, (step, other) in enumerate(blocks[1:], 1):
            steps = jnp.where(block == index, step, steps)
            twin = jnp.where(block == index, other, twin)
        base = within + divided(within, CAP) * CAP
        for ref, holder in zip(pair, (place_ref[1], 1 - place_ref[1])):
            layer = (place_ref[0] + steps * (2 * holder - 1)) & 7
            core = holder + twin * (1 - 2 * holder)
            places.append((ref, layer * (8 * CAP) + core * CAP + base))
    for start in range(0, out.shape[1], 256):
        total = jnp.zeros((units, 256), F32)
        for ref, target in places:
            column = lax.broadcasted_iota(jnp.int32, (ref.shape[1], 256), 1) + start
            table = jnp.where(column == target, 1.0, 0.0).astype(BF16)
            total = total + jnp.dot(ref[...], table, preferred_element_type=F32)
        out[:, start : start + 256] = total.astype(BF16)
    copy = pltpu.make_async_copy(out, out_ref, sems.at[0])
    copy.start()
    copy.wait()


def last(place, blocks, pair, mine_early, other_early, other_late):
    units, count = pair[0].shape[0], 3 * blocks[0].shape[0]
    out = shape((units, 1280), BF16)
    return pl.pallas_call(
        last_kernel,
        out_shape=out,
        in_specs=[SMEM] + [WHOLE] * 8,
        out_specs=WHOLE,
        scratch_shapes=[
            pltpu.VMEM((count, 4096), BF16),
            pltpu.VMEM((2 * units, 4096), BF16),
            pltpu.VMEM(mine_early.shape, BF16),
            pltpu.VMEM(other_early.shape, BF16),
            pltpu.VMEM((units, count), BF16),
            pltpu.VMEM((units, count), BF16),
            pltpu.VMEM(out.shape, BF16),
            pltpu.SemaphoreType.DMA((8,)),
        ],
        name="last",
        compiler_params=pltpu.CompilerParams(vmem_limit_bytes=60 << 20),
        cost_estimate=pl.CostEstimate(flops=1 << 30, transcendentals=0, bytes_accessed=8 << 20),
    )(place, *blocks, *pair, mine_early, other_early, other_late)


def silu(value):
    return value / (1.0 + jnp.exp(-value))


def softplus(value):
    small = jnp.exp(-jnp.abs(value))
    ratio = small / (2.0 + small)
    square = ratio * ratio
    series = jnp.full_like(square, 1.0 / 15.0)
    for odd in (13, 11, 9, 7, 5, 3):
        series = series * square + 1.0 / odd
    return jnp.maximum(value, 0.0) + 2.0 * ratio * (series * square + 1.0)


def conv_kernel(
    x_ref,
    rim_ref,
    raw_ref,
    weight_ref,
    proj_ref,
    bias_ref,
    decay_ref,
    conv_ref,
    step_ref,
    drive_ref,
    rate_ref,
    part_ref,
    padded,
):
    rows, width = x_ref.shape
    padded[8:, :] = x_ref[...].astype(F32)
    padded[5:8, :] = rim_ref[...].astype(F32)
    total = jnp.zeros((rows, width), F32)
    for tap in range(4):
        total = total + weight_ref[tap : tap + 1, :] * padded[5 + tap : 5 + tap + rows, :]
    conv = silu(total)
    conv_ref[...] = conv
    part = lax.dot_general(
        proj_ref[...], conv.astype(BF16), (((1,), (1,)), ((), ())), preferred_element_type=F32
    )
    for index in range(8):
        part_ref[index] = part
    step = softplus(raw_ref[...].astype(F32) + bias_ref[...])
    drive = step * conv
    rate = -jnp.exp(decay_ref[...]) * LOG2E
    for index in range(width // 128):
        lanes = slice(index * 128, index * 128 + 128)
        step_ref[pl.ds(index, rows, stride=8), :] = step[:, lanes]
        drive_ref[pl.ds(index, rows, stride=8), :] = drive[:, lanes]
        rate_ref[pl.ds(index, rate.shape[0], stride=8), :] = rate[:, lanes]


def pack_state(states, total):
    high = total.astype(BF16).astype(F32)
    middle = (total - high).astype(BF16).astype(F32)
    low = total - high - middle
    tail = jnp.concatenate([high, middle, low, jnp.zeros_like(total)], axis=0)
    return jnp.concatenate(list(states) + [tail], axis=0).astype(BF16)


def unpack_state(ref, position):
    block = ref[position].astype(F32)
    states = [block[n * 8 : n * 8 + 8] for n in range(16)]
    return states, block[128:136] + block[136:144] + block[144:152]


def scan_kernel(coef_ref, step_ref, drive_ref, rate_ref, y_ref, sum_ref, end_ref):
    rows = step_ref.shape[0] // 8
    rates = [rate_ref[n * 8 : n * 8 + 8, :] for n in range(16)]
    zero = jnp.zeros((8, 128), F32)

    def advance(token, carry):
        total, states = carry
        here = pl.ds(pl.multiple_of(token * 8, 8), 8)
        step, drive = step_ref[here, :], drive_ref[here, :]
        total = total + step
        sum_ref[here, :] = total
        parts, following = [zero, zero], []
        for n in range(16):
            state = jnp.exp2(rates[n] * step) * states[n] + coef_ref[n, token] * drive
            parts[n % 2] = parts[n % 2] + coef_ref[16 + n, token] * state
            following.append(state)
        y_ref[here, :] = parts[0] + parts[1]
        return total, tuple(following)

    total, states = lax.fori_loop(0, rows, advance, (zero, (zero,) * 16), unroll=4)
    packed = pack_state(states, total)
    for index in range(8):
        end_ref[index] = packed


def fold(ref, rates, limit, states, total):
    for position in range(8):
        more, step = unpack_state(ref, position)
        keep = position < limit
        states = [
            jnp.where(keep, jnp.exp2(rates[n] * step) * states[n] + more[n], states[n])
            for n in range(16)
        ]
        total = jnp.where(keep, total + step, total)
    return states, total


def group_kernel(mine_ref, got_ref, rate_ref, before_ref, step_ref, all_ref):
    rates = [rate_ref[n * 8 : n * 8 + 8, :] for n in range(16)]
    zero = jnp.zeros((8, 128), F32)
    states, total = fold(got_ref, rates, mine_ref[0], [zero] * 16, zero)
    for n in range(16):
        before_ref[n * 8 : n * 8 + 8, :] = states[n]
    step_ref[...] = total
    states, total = fold(got_ref, rates, 8, [zero] * 16, zero)
    packed = pack_state(states, total)
    for index in range(8):
        all_ref[index] = packed


def finish_kernel(
    mine_ref,
    coef_ref,
    got_ref,
    rate_ref,
    before_ref,
    before_step_ref,
    y_ref,
    sum_ref,
    conv_ref,
    gain_ref,
    z_ref,
    out_ref,
    dense,
):
    rows, width = conv_ref.shape
    rates = [rate_ref[n * 8 : n * 8 + 8, :] for n in range(16)]
    zero = jnp.zeros((8, 128), F32)
    states, _ = fold(got_ref, rates, mine_ref[0], [zero] * 16, zero)
    states = [
        jnp.exp2(rates[n] * before_step_ref[...]) * states[n] + before_ref[n * 8 : n * 8 + 8, :]
        for n in range(16)
    ]

    def advance(token, carry):
        here = pl.ds(pl.multiple_of(token * 8, 8), 8)
        total = sum_ref[here, :]
        parts = [y_ref[here, :], zero]
        for n in range(16):
            parts[n % 2] = parts[n % 2] + coef_ref[16 + n, token] * (
                jnp.exp2(rates[n] * total) * states[n]
            )
        dense[here, :] = parts[0] + parts[1]
        return carry

    lax.fori_loop(0, rows, advance, 0, unroll=4)
    for index in range(width // 128):
        lanes = slice(index * 128, index * 128 + 128)
        value = dense[pl.ds(index, rows, stride=8), :]
        value = value + gain_ref[:, lanes] * conv_ref[:, lanes]
        out_ref[:, lanes] = (value * silu(z_ref[:, lanes].astype(F32))).astype(BF16)


def shards(
    inner_x,
    inner_z,
    step_raw,
    conv_weight,
    state_proj,
    step_bias,
    decay_log,
    skip_gain,
    moe_tokens,
    routes,
    gate_weight,
    up_weight,
):
    rows, width = inner_x.shape
    shards_of = lax.axis_size(SEQ)
    rim = lax.ppermute(inner_x[rows - 3 :], SEQ, [(i, i + 1) for i in range(shards_of - 1)])
    swap = [(0, 1), (1, 0)]
    features = moe_tokens.shape[1]
    placed = call(
        place_kernel,
        shape((32, 2 * CAP, features // 2), BF16),
        [WHOLE] * 2,
        [pltpu.VMEM((2 * CAP, features // 2), F32)],
        name="place",
        flops=1 << 28,
    )(routes.T, moe_tokens)
    arrived = lax.all_to_all(placed, ("exp", "x"), split_axis=0, concat_axis=0, tiled=True)
    dense = shape((rows * width // 128, 128), F32)
    conv, step, drive, rate, part = call(
        conv_kernel,
        (
            shape((rows, width), F32),
            dense,
            dense,
            shape((128, 128), F32),
            shape((8, 32, rows), F32),
        ),
        [WHOLE] * 7,
        [pltpu.VMEM((rows + 8, width), F32)],
        name="conv", flops=1 << 29,
    )(inner_x, rim, step_raw, conv_weight, state_proj.T, step_bias[None], decay_log)
    dense = shape((rows * width // 128, 128), F32)
    conv, step, drive, rate, part = call(
        conv_kernel,
        (
            shape((rows, width), F32),
            dense,
            dense,
            shape((128, 128), F32),
            shape((8, 32, rows), F32),
        ),
        [WHOLE] * 7,
        [pltpu.VMEM((rows + 8, width), F32)],
        name="conv", flops=1 << 29,
    )(inner_x, rim, step_raw, conv_weight, state_proj.T, step_bias[None], decay_log)
    weight = jnp.concatenate([gate_weight[0], up_weight[0]], axis=0)
    weights = gate_weight[0], up_weight[0]
    others = [lax.ppermute(weight, "c", swap) for weight in weights]
    arrived, part, *others = lax.optimization_barrier((arrived, part, *others))
    pairs = [others, weights]
    block = call(
        assemble_kernel,
        shape((4 * CAP, 4096), BF16),
        [WHOLE],
        [pltpu.VMEM((4 * CAP, 4096), F32)],
        name="assemble",
        vmem=16,
        flops=1 << 28,
    )(arrived)
    onward = [(2 * z + c, 2 * ((z + 1 - 2 * c) % 8) + c) for z in range(8) for c in range(2)]

    def step_on(rows):
        return lax.ppermute(rows, ("z", "c"), onward)

    own, twin = [block, step_on(block)], [lax.ppermute(block, "c", swap)]
    twin[0], part = lax.optimization_barrier((twin[0], part))
    twin.append(step_on(twin[0]))
    coef = lax.all_to_all(part, "exp", split_axis=0, concat_axis=0, tiled=True)
    own[1], coef = lax.optimization_barrier((own[1], coef))
    coef = jnp.sum(coef, axis=0)
    packed = shape((8, 160, 128), BF16)
    local, sums, ends = call(
        scan_kernel, (dense, dense, packed), [SMEM] + [WHOLE] * 3, name="scan", flops=1 << 31
    )(coef, step, drive, rate)
    own.append(step_on(own[1]))
    twin.append(step_on(twin[1]))
    own[2], _ = lax.optimization_barrier((own[2], ends))
    own.append(step_on(own[2]))
    twin.append(step_on(twin[2]))
    own.append(step_on(own[3]))
    near = lax.all_to_all(ends, ("x", "c"), split_axis=0, concat_axis=0, tiled=True)
    place_in = lax.axis_index(("x", "c")).astype(jnp.int32).reshape(1)
    before, before_step, whole = call(
        group_kernel,
        (shape((128, 128), F32), shape((8, 128), F32), packed),
        [SMEM, WHOLE, WHOLE],
        name="group", vmem=16, flops=1 << 28,
    )(place_in, near, rate)
    far = lax.all_to_all(whole, "z", split_axis=0, concat_axis=0, tiled=True)
    layer = lax.axis_index("z").astype(jnp.int32).reshape(1)
    mixed = call(
        finish_kernel,
        shape((rows, width), BF16),
        [SMEM, SMEM] + [WHOLE] * 9,
        [pltpu.VMEM(dense.shape, F32)],
        name="finish", flops=1 << 31,
    )(layer, coef, far, rate, before, before_step, local, sums, conv, skip_gain[None], inner_z)

    other_early, mine_early = expand([block, own[1], twin[1], own[2], twin[2]], pairs, "expand_early")
    late = [own[3], twin[3], own[4]]
    (other_late,) = expand(late, pairs[:1], "expand_other")
    other_early, other_late = (lax.ppermute(part, "c", swap) for part in (other_early, other_late))
    here = jnp.stack([lax.axis_index("z"), lax.axis_index("c")]).astype(jnp.int32)
    other_late, mixed = lax.optimization_barrier((other_late, mixed))
    hidden = last(here, late, weights, mine_early, other_early, other_late)[None]
    return mixed, hidden


def solution(mesh):
    fine = Mesh(mesh.devices.reshape(8, 4, 2, 8), ("z", "x", "c", "exp"))
    return jax.shard_map(
        shards,
        mesh=fine,
        in_specs=(
            P(SEQ, "exp"),
            P(SEQ, "exp"),
            P(SEQ, "exp"),
            P(None, "exp"),
            P("exp", None),
            P("exp"),
            P(None, "exp"),
            P("exp"),
            P(SEQ, "exp"),
            P(SEQ, None),
            P("exp", SEQ, None),
            P("exp", SEQ, None),
        ),
        out_specs=(P(SEQ, "exp"), P("exp", SEQ, None)),
        check_vma=False,
    )
```

```python
import functools

import jax
import jax.numpy as jnp
from jax import lax
from jax.experimental import pallas as pl
from jax.experimental.pallas import tpu as pltpu
from jax.sharding import Mesh
from jax.sharding import PartitionSpec as P

CAP = 20
F32 = jnp.float32
BF16 = jnp.bfloat16
LOG2E = 1.4426950408889634
SEQ = ("z", "x", "c")

VMEM = pl.BlockSpec(memory_space=pltpu.VMEM)
SMEM = pl.BlockSpec(memory_space=pltpu.SMEM)
WHOLE = pl.BlockSpec(memory_space=pltpu.HBM)


def call(kernel, out_shape, in_specs, scratch=(), name=None, vmem=60, flops=0, lazy=False):
    single = not isinstance(out_shape, tuple)
    outs = (out_shape,) if single else out_shape

    def run(*operands):
        moved = [index for index in range(len(in_specs)) if in_specs[index] is WHOLE]
        buffers = [pltpu.VMEM(operands[index].shape, operands[index].dtype) for index in moved]
        buffers += [pltpu.VMEM(out.shape, out.dtype) for out in outs]
        count = len(operands)

        def body(*refs):
            inputs, results = list(refs[:count]), refs[count : count + len(outs)]
            held = refs[count + len(outs) : count + len(outs) + len(buffers)]
            rest, sems = refs[count + len(outs) + len(buffers) : -1], refs[-1]
            copies = []
            for place, index in enumerate(moved):
                copies.append(pltpu.make_async_copy(inputs[index], held[place], sems.at[place]))
                inputs[index] = held[place]
            for copy in copies:
                copy.start()
            made = held[len(moved) :]
            if lazy:
                kernel(copies, *inputs, *made, *rest)
            else:
                for copy in copies:
                    copy.wait()
                kernel(*inputs, *made, *rest)
            copies = [
                pltpu.make_async_copy(source, target, sems.at[len(moved) + place])
                for place, (source, target) in enumerate(zip(made, results))
            ]
            for copy in copies:
                copy.start()
            for copy in copies:
                copy.wait()

        found = pl.pallas_call(
            body,
            out_shape=outs,
            in_specs=in_specs,
            out_specs=(WHOLE,) * len(outs),
            scratch_shapes=[*buffers, *scratch, pltpu.SemaphoreType.DMA((len(buffers),))],
            name=name,
            compiler_params=pltpu.CompilerParams(vmem_limit_bytes=vmem << 20),
            cost_estimate=pl.CostEstimate(flops=flops, transcendentals=0, bytes_accessed=4 << 20),
        )(*operands)
        return found[0] if single else found

    return run


def shape(dims, dtype):
    return jax.ShapeDtypeStruct(dims, dtype)


def place_kernel(routes_ref, tokens_ref, out_ref, wide):
    tokens = tokens_ref.shape[0]
    row = lax.broadcasted_iota(jnp.int32, (256, tokens), 0)
    expert, slot = row >> 5, row & 31
    named = (routes_ref[0:1, :] == expert) | (routes_ref[1:2, :] == expert)
    earlier = lax.broadcasted_iota(jnp.int32, (tokens, tokens), 0) < lax.broadcasted_iota(
        jnp.int32, (tokens, tokens), 1
    )
    before = jnp.dot(
        jnp.where(named, 1.0, 0.0).astype(BF16),
        jnp.where(earlier, 1.0, 0.0).astype(BF16),
        preferred_element_type=F32,
    )
    table = jnp.where(named & (before == slot.astype(F32)), 1.0, 0.0).astype(BF16)
    placed = jnp.dot(table, tokens_ref[...], preferred_element_type=F32)
    for index in range(8):
        rows = placed[index * 32 : index * 32 + CAP]
        wide[:CAP, :], wide[CAP:, :] = rows[:, :256], rows[:, 256:]
        packed = wide[...].astype(BF16)
        for copy in range(4):
            out_ref[index * 4 + copy] = packed


def assemble_kernel(got_ref, out_ref, wide):
    for index in range(32):
        rows = got_ref[index].astype(F32)
        here = pl.ds(index % 4 * CAP, CAP)
        start = index // 4 * 512
        wide[here, start : start + 256] = rows[:CAP]
        wide[here, start + 256 : start + 512] = rows[CAP:]
    out_ref[...] = wide[...].astype(BF16)


def expand_kernel(blocks, pairs, *refs):
    inputs = blocks + 2 * pairs
    sources, outs, refs = refs[:inputs], refs[inputs : inputs + pairs], refs[inputs + pairs :]
    rows, held, made, sems = refs[0], refs[1 : 1 + pairs], refs[1 + pairs : -1], refs[-1]
    copies, start = [], 0
    for source in sources[:blocks]:
        size = source.shape[0]
        copies.append((source, rows.at[pl.ds(start, size)]))
        start += size
    units = made[0].shape[0]
    for index, source in enumerate(sources[blocks:]):
        target = held[index // 2].at[pl.ds(index % 2 * units, units)]
        copies.append((source, target))
    copies = [
        pltpu.make_async_copy(source, target, sems.at[index])
        for index, (source, target) in enumerate(copies)
    ]
    for copy in copies:
        copy.start()
    for copy in copies[:blocks]:
        copy.wait()
    sent = []
    for index, (weight, hidden, out) in enumerate(zip(held, made, outs)):
        for copy in copies[blocks + 2 * index : blocks + 2 * index + 2]:
            copy.wait()
        both = lax.dot_general(
            weight[...], rows[...], (((1,), (1,)), ((), ())), preferred_element_type=F32
        )
        hidden[...] = (silu(both[:units]) * both[units:]).astype(BF16)
        sent.append(pltpu.make_async_copy(hidden, out, sems.at[inputs + index]))
        sent[-1].start()
    for copy in sent:
        copy.wait()


def expand(blocks, pairs, name):
    weights = [weight for pair in pairs for weight in pair]
    units, count = weights[0].shape[0], sum(block.shape[0] for block in blocks)
    out = shape((units, count), BF16)
    total = len(pairs)
    return pl.pallas_call(
        functools.partial(expand_kernel, len(blocks), total),
        out_shape=(out,) * total,
        in_specs=[WHOLE] * (len(blocks) + 2 * total),
        out_specs=(WHOLE,) * total,
        scratch_shapes=[
            pltpu.VMEM((count, 4096), BF16),
            *[pltpu.VMEM((2 * units, 4096), BF16)] * total,
            *[pltpu.VMEM(out.shape, BF16)] * total,
            pltpu.SemaphoreType.DMA((len(blocks) + 3 * total,)),
        ],
        name=name,
        compiler_params=pltpu.CompilerParams(vmem_limit_bytes=60 << 20),
        cost_estimate=pl.CostEstimate(
            flops=4 * total * units * count * 4096, transcendentals=0, bytes_accessed=8 << 20
        ),
    )(*blocks, *weights)


def divided(value, by):
    return (value * (65536 // by + 1)) >> 16


EARLY = ((0, 0), (1, 0), (1, 1), (2, 0), (2, 1))
LATE = ((3, 0), (3, 1), (4, 0))


def last_kernel(place_ref, *refs):
    (*sources, out_ref), held = refs[:9], refs[9:-1]
    rows, weight, mine_early, other_early, other_late, mine_late, out, sems = *held, refs[-1]
    size, units = sources[0].shape[0], sources[3].shape[0]
    targets = [rows.at[pl.ds(index * size, size)] for index in range(3)]
    targets += [weight.at[pl.ds(index * units, units)] for index in range(2)]
    targets += [mine_early, other_early, other_late]
    copies = [
        pltpu.make_async_copy(source, target, sems.at[index])
        for index, (source, target) in enumerate(zip(sources, targets))
    ]
    for copy in copies[5:] + copies[:5]:
        copy.start()

    def ordered(pair, blocks, first):
        count = pair[0].shape[1]
        row = lax.broadcasted_iota(jnp.int32, (count, 1), 0)
        block = divided(row, 4 * CAP)
        within = row - block * (4 * CAP)
        steps, twin = (jnp.full_like(row, value) for value in blocks[0])
        for index, (step, other) in enumerate(blocks[1:], 1):
            steps = jnp.where(block == index, step, steps)
            twin = jnp.where(block == index, other, twin)
        base = within + divided(within, CAP) * CAP
        places = []
        for ref, holder in zip(pair, (place_ref[1], 1 - place_ref[1])):
            layer = (place_ref[0] + steps * (2 * holder - 1)) & 7
            core = holder + twin * (1 - 2 * holder)
            places.append((ref, layer * (8 * CAP) + core * CAP + base))
        for start in range(0, out.shape[1], 256):
            here = slice(start, start + 256)
            total = jnp.zeros((units, 256), F32) if first else out[:, here].astype(F32)
            for ref, target in places:
                column = lax.broadcasted_iota(jnp.int32, (count, 256), 1) + start
                table = jnp.where(column == target, 1.0, 0.0).astype(BF16)
                total = total + jnp.dot(ref[...], table, preferred_element_type=F32)
            out[:, here] = total.astype(BF16)

    for copy in copies[5:7]:
        copy.wait()
    ordered((mine_early, other_early), EARLY, True)
    for copy in copies[7:] + copies[:5]:
        copy.wait()
    both = lax.dot_general(
        weight[...], rows[...], (((1,), (1,)), ((), ())), preferred_element_type=F32
    )
    mine_late[...] = (silu(both[:units]) * both[units:]).astype(BF16)
    ordered((mine_late, other_late), LATE, False)
    copy = pltpu.make_async_copy(out, out_ref, sems.at[0])
    copy.start()
    copy.wait()


def last(place, blocks, pair, mine_early, other_early, other_late):
    units, count = pair[0].shape[0], 3 * blocks[0].shape[0]
    out = shape((units, 1280), BF16)
    return pl.pallas_call(
        last_kernel,
        out_shape=out,
        in_specs=[SMEM] + [WHOLE] * 8,
        out_specs=WHOLE,
        scratch_shapes=[
            pltpu.VMEM((count, 4096), BF16),
            pltpu.VMEM((2 * units, 4096), BF16),
            pltpu.VMEM(mine_early.shape, BF16),
            pltpu.VMEM(other_early.shape, BF16),
            pltpu.VMEM((units, count), BF16),
            pltpu.VMEM((units, count), BF16),
            pltpu.VMEM(out.shape, BF16),
            pltpu.SemaphoreType.DMA((8,)),
        ],
        name="last",
        compiler_params=pltpu.CompilerParams(vmem_limit_bytes=60 << 20),
        cost_estimate=pl.CostEstimate(flops=1 << 30, transcendentals=0, bytes_accessed=8 << 20),
    )(place, *blocks, *pair, mine_early, other_early, other_late)


def silu(value):
    return value / (1.0 + jnp.exp(-value))


def softplus(value):
    small = jnp.exp(-jnp.abs(value))
    ratio = small / (2.0 + small)
    square = ratio * ratio
    series = jnp.full_like(square, 1.0 / 15.0)
    for odd in (13, 11, 9, 7, 5, 3):
        series = series * square + 1.0 / odd
    return jnp.maximum(value, 0.0) + 2.0 * ratio * (series * square + 1.0)


def conv_kernel(
    x_ref,
    rim_ref,
    raw_ref,
    weight_ref,
    proj_ref,
    bias_ref,
    decay_ref,
    conv_ref,
    step_ref,
    drive_ref,
    rate_ref,
    part_ref,
    padded,
):
    rows, width = x_ref.shape
    padded[8:, :] = x_ref[...].astype(F32)
    padded[5:8, :] = rim_ref[...].astype(F32)
    total = jnp.zeros((rows, width), F32)
    for tap in range(4):
        total = total + weight_ref[tap : tap + 1, :] * padded[5 + tap : 5 + tap + rows, :]
    conv = silu(total)
    conv_ref[...] = conv
    part = lax.dot_general(
        proj_ref[...], conv.astype(BF16), (((1,), (1,)), ((), ())), preferred_element_type=F32
    )
    for index in range(8):
        part_ref[index] = part
    step = softplus(raw_ref[...].astype(F32) + bias_ref[...])
    drive = step * conv
    rate = -jnp.exp(decay_ref[...]) * LOG2E
    for index in range(width // 128):
        lanes = slice(index * 128, index * 128 + 128)
        step_ref[pl.ds(index, rows, stride=8), :] = step[:, lanes]
        drive_ref[pl.ds(index, rows, stride=8), :] = drive[:, lanes]
        rate_ref[pl.ds(index, rate.shape[0], stride=8), :] = rate[:, lanes]


def pack_state(states, total):
    high = total.astype(BF16).astype(F32)
    middle = (total - high).astype(BF16).astype(F32)
    low = total - high - middle
    tail = jnp.concatenate([high, middle, low, jnp.zeros_like(total)], axis=0)
    return jnp.concatenate(list(states) + [tail], axis=0).astype(BF16)


def unpack_state(ref, position):
    block = ref[position].astype(F32)
    states = [block[n * 8 : n * 8 + 8] for n in range(16)]
    return states, block[128:136] + block[136:144] + block[144:152]


def scan_kernel(coef_ref, step_ref, drive_ref, rate_ref, y_ref, sum_ref, end_ref):
    rows = step_ref.shape[0] // 8
    rates = [rate_ref[n * 8 : n * 8 + 8, :] for n in range(16)]
    zero = jnp.zeros((8, 128), F32)

    def advance(token, carry):
        total, states = carry
        here = pl.ds(pl.multiple_of(token * 8, 8), 8)
        step, drive = step_ref[here, :], drive_ref[here, :]
        total = total + step
        sum_ref[here, :] = total
        parts, following = [zero, zero], []
        for n in range(16):
            state = jnp.exp2(rates[n] * step) * states[n] + coef_ref[n, token] * drive
            parts[n % 2] = parts[n % 2] + coef_ref[16 + n, token] * state
            following.append(state)
        y_ref[here, :] = parts[0] + parts[1]
        return total, tuple(following)

    total, states = lax.fori_loop(0, rows, advance, (zero, (zero,) * 16), unroll=4)
    packed = pack_state(states, total)
    for index in range(8):
        end_ref[index] = packed


def fold(ref, rates, limit, states, total):
    for position in range(8):
        more, step = unpack_state(ref, position)
        keep = position < limit
        states = [
            jnp.where(keep, jnp.exp2(rates[n] * step) * states[n] + more[n], states[n])
            for n in range(16)
        ]
        total = jnp.where(keep, total + step, total)
    return states, total


def group_kernel(mine_ref, got_ref, rate_ref, before_ref, step_ref, all_ref):
    rates = [rate_ref[n * 8 : n * 8 + 8, :] for n in range(16)]
    zero = jnp.zeros((8, 128), F32)
    states, total = fold(got_ref, rates, mine_ref[0], [zero] * 16, zero)
    for n in range(16):
        before_ref[n * 8 : n * 8 + 8, :] = states[n]
    step_ref[...] = total
    states, total = fold(got_ref, rates, 8, [zero] * 16, zero)
    packed = pack_state(states, total)
    for index in range(8):
        all_ref[index] = packed


def finish_kernel(
    copies,
    mine_ref,
    coef_ref,
    got_ref,
    rate_ref,
    before_ref,
    before_step_ref,
    y_ref,
    sum_ref,
    conv_ref,
    gain_ref,
    z_ref,
    out_ref,
    dense,
):
    rows, width = conv_ref.shape
    for copy in copies[:4]:
        copy.wait()
    rates = [rate_ref[n * 8 : n * 8 + 8, :] for n in range(16)]
    zero = jnp.zeros((8, 128), F32)
    states, _ = fold(got_ref, rates, mine_ref[0], [zero] * 16, zero)
    states = [
        jnp.exp2(rates[n] * before_step_ref[...]) * states[n] + before_ref[n * 8 : n * 8 + 8, :]
        for n in range(16)
    ]

    for copy in copies[4:6]:
        copy.wait()

    def advance(token, carry):
        here = pl.ds(pl.multiple_of(token * 8, 8), 8)
        total = sum_ref[here, :]
        parts = [y_ref[here, :], zero]
        for n in range(16):
            parts[n % 2] = parts[n % 2] + coef_ref[16 + n, token] * (
                jnp.exp2(rates[n] * total) * states[n]
            )
        dense[here, :] = parts[0] + parts[1]
        return carry

    lax.fori_loop(0, rows, advance, 0, unroll=4)
    for copy in copies[6:]:
        copy.wait()
    for index in range(width // 128):
        lanes = slice(index * 128, index * 128 + 128)
        value = dense[pl.ds(index, rows, stride=8), :]
        value = value + gain_ref[:, lanes] * conv_ref[:, lanes]
        out_ref[:, lanes] = (value * silu(z_ref[:, lanes].astype(F32))).astype(BF16)


def shards(
    inner_x,
    inner_z,
    step_raw,
    conv_weight,
    state_proj,
    step_bias,
    decay_log,
    skip_gain,
    moe_tokens,
    routes,
    gate_weight,
    up_weight,
):
    rows, width = inner_x.shape
    shards_of = lax.axis_size(SEQ)
    rim = lax.ppermute(inner_x[rows - 3 :], SEQ, [(i, i + 1) for i in range(shards_of - 1)])
    swap = [(0, 1), (1, 0)]
    features = moe_tokens.shape[1]
    placed = call(
        place_kernel,
        shape((32, 2 * CAP, features // 2), BF16),
        [WHOLE] * 2,
        [pltpu.VMEM((2 * CAP, features // 2), F32)],
        name="place",
        flops=1 << 28,
    )(routes.T, moe_tokens)
    arrived = lax.all_to_all(placed, ("exp", "x"), split_axis=0, concat_axis=0, tiled=True)
    dense = shape((rows * width // 128, 128), F32)
    conv, step, drive, rate, part = call(
        conv_kernel,
        (
            shape((rows, width), F32),
            dense,
            dense,
            shape((128, 128), F32),
            shape((8, 32, rows), F32),
        ),
        [WHOLE] * 7,
        [pltpu.VMEM((rows + 8, width), F32)],
        name="conv", flops=1 << 29,
    )(inner_x, rim, step_raw, conv_weight, state_proj.T, step_bias[None], decay_log)
    dense = shape((rows * width // 128, 128), F32)
    conv, step, drive, rate, part = call(
        conv_kernel,
        (
            shape((rows, width), F32),
            dense,
            dense,
            shape((128, 128), F32),
            shape((8, 32, rows), F32),
        ),
        [WHOLE] * 7,
        [pltpu.VMEM((rows + 8, width), F32)],
        name="conv", flops=1 << 29,
    )(inner_x, rim, step_raw, conv_weight, state_proj.T, step_bias[None], decay_log)
    weight = jnp.concatenate([gate_weight[0], up_weight[0]], axis=0)
    weights = gate_weight[0], up_weight[0]
    others = [lax.ppermute(weight, "c", swap) for weight in weights]
    arrived, part, *others = lax.optimization_barrier((arrived, part, *others))
    pairs = [others, weights]
    block = call(
        assemble_kernel,
        shape((4 * CAP, 4096), BF16),
        [WHOLE],
        [pltpu.VMEM((4 * CAP, 4096), F32)],
        name="assemble",
        vmem=16,
        flops=1 << 28,
    )(arrived)
    onward = [(2 * z + c, 2 * ((z + 1 - 2 * c) % 8) + c) for z in range(8) for c in range(2)]

    def step_on(rows):
        return lax.ppermute(rows, ("z", "c"), onward)

    own, twin = [block, step_on(block)], [lax.ppermute(block, "c", swap)]
    twin[0], part = lax.optimization_barrier((twin[0], part))
    twin.append(step_on(twin[0]))
    coef = lax.all_to_all(part, "exp", split_axis=0, concat_axis=0, tiled=True)
    own[1], coef = lax.optimization_barrier((own[1], coef))
    coef = jnp.sum(coef, axis=0)
    packed = shape((8, 160, 128), BF16)
    local, sums, ends = call(
        scan_kernel, (dense, dense, packed), [SMEM] + [WHOLE] * 3, name="scan", flops=1 << 31
    )(coef, step, drive, rate)
    own.append(step_on(own[1]))
    twin.append(step_on(twin[1]))
    own[2], _ = lax.optimization_barrier((own[2], ends))
    own.append(step_on(own[2]))
    twin.append(step_on(twin[2]))
    own.append(step_on(own[3]))
    near = lax.all_to_all(ends, ("x", "c"), split_axis=0, concat_axis=0, tiled=True)
    place_in = lax.axis_index(("x", "c")).astype(jnp.int32).reshape(1)
    before, before_step, whole = call(
        group_kernel,
        (shape((128, 128), F32), shape((8, 128), F32), packed),
        [SMEM, WHOLE, WHOLE],
        name="group", vmem=16, flops=1 << 28,
    )(place_in, near, rate)
    far = lax.all_to_all(whole, "z", split_axis=0, concat_axis=0, tiled=True)
    layer = lax.axis_index("z").astype(jnp.int32).reshape(1)
    mixed = call(
        finish_kernel,
        shape((rows, width), BF16),
        [SMEM, SMEM] + [WHOLE] * 9,
        [pltpu.VMEM(dense.shape, F32)],
        lazy=True, name="finish", flops=1 << 31,
    )(layer, coef, far, rate, before, before_step, local, sums, conv, skip_gain[None], inner_z)

    other_early, mine_early = expand([block, own[1], twin[1], own[2], twin[2]], pairs, "expand_early")
    late = [own[3], twin[3], own[4]]
    (other_late,) = expand(late, pairs[:1], "expand_other")
    other_early, other_late = (lax.ppermute(part, "c", swap) for part in (other_early, other_late))
    here = jnp.stack([lax.axis_index("z"), lax.axis_index("c")]).astype(jnp.int32)
    other_late, mixed = lax.optimization_barrier((other_late, mixed))
    hidden = last(here, late, weights, mine_early, other_early, other_late)[None]
    return mixed, hidden


def solution(mesh):
    fine = Mesh(mesh.devices.reshape(8, 4, 2, 8), ("z", "x", "c", "exp"))
    return jax.shard_map(
        shards,
        mesh=fine,
        in_specs=(
            P(SEQ, "exp"),
            P(SEQ, "exp"),
            P(SEQ, "exp"),
            P(None, "exp"),
            P("exp", None),
            P("exp"),
            P(None, "exp"),
            P("exp"),
            P(SEQ, "exp"),
            P(SEQ, None),
            P("exp", SEQ, None),
            P("exp", SEQ, None),
        ),
        out_specs=(P(SEQ, "exp"), P("exp", SEQ, None)),
        check_vma=False,
    )
```

```python
import functools

import jax
import jax.numpy as jnp
from jax import lax
from jax.experimental import pallas as pl
from jax.experimental.pallas import tpu as pltpu
from jax.sharding import Mesh
from jax.sharding import PartitionSpec as P

CAP = 20
F32 = jnp.float32
BF16 = jnp.bfloat16
LOG2E = 1.4426950408889634
SEQ = ("z", "x", "c")

VMEM = pl.BlockSpec(memory_space=pltpu.VMEM)
SMEM = pl.BlockSpec(memory_space=pltpu.SMEM)
WHOLE = pl.BlockSpec(memory_space=pltpu.HBM)


def call(kernel, out_shape, in_specs, scratch=(), name=None, vmem=60, flops=0, lazy=False):
    single = not isinstance(out_shape, tuple)
    outs = (out_shape,) if single else out_shape

    def run(*operands):
        moved = [index for index in range(len(in_specs)) if in_specs[index] is WHOLE]
        buffers = [pltpu.VMEM(operands[index].shape, operands[index].dtype) for index in moved]
        buffers += [pltpu.VMEM(out.shape, out.dtype) for out in outs]
        count = len(operands)

        def body(*refs):
            inputs, results = list(refs[:count]), refs[count : count + len(outs)]
            held = refs[count + len(outs) : count + len(outs) + len(buffers)]
            rest, sems = refs[count + len(outs) + len(buffers) : -1], refs[-1]
            copies = []
            for place, index in enumerate(moved):
                copies.append(pltpu.make_async_copy(inputs[index], held[place], sems.at[place]))
                inputs[index] = held[place]
            for copy in copies:
                copy.start()
            made = held[len(moved) :]
            if lazy:
                kernel(copies, *inputs, *made, *rest)
            else:
                for copy in copies:
                    copy.wait()
                kernel(*inputs, *made, *rest)
            copies = [
                pltpu.make_async_copy(source, target, sems.at[len(moved) + place])
                for place, (source, target) in enumerate(zip(made, results))
            ]
            for copy in copies:
                copy.start()
            for copy in copies:
                copy.wait()

        found = pl.pallas_call(
            body,
            out_shape=outs,
            in_specs=in_specs,
            out_specs=(WHOLE,) * len(outs),
            scratch_shapes=[*buffers, *scratch, pltpu.SemaphoreType.DMA((len(buffers),))],
            name=name,
            compiler_params=pltpu.CompilerParams(vmem_limit_bytes=vmem << 20),
            cost_estimate=pl.CostEstimate(flops=flops, transcendentals=0, bytes_accessed=4 << 20),
        )(*operands)
        return found[0] if single else found

    return run


def shape(dims, dtype):
    return jax.ShapeDtypeStruct(dims, dtype)


def place_kernel(routes_ref, tokens_ref, out_ref, wide):
    tokens = tokens_ref.shape[0]
    row = lax.broadcasted_iota(jnp.int32, (256, tokens), 0)
    expert, slot = row >> 5, row & 31
    named = (routes_ref[0:1, :] == expert) | (routes_ref[1:2, :] == expert)
    earlier = lax.broadcasted_iota(jnp.int32, (tokens, tokens), 0) < lax.broadcasted_iota(
        jnp.int32, (tokens, tokens), 1
    )
    before = jnp.dot(
        jnp.where(named, 1.0, 0.0).astype(BF16),
        jnp.where(earlier, 1.0, 0.0).astype(BF16),
        preferred_element_type=F32,
    )
    table = jnp.where(named & (before == slot.astype(F32)), 1.0, 0.0).astype(BF16)
    placed = jnp.dot(table, tokens_ref[...], preferred_element_type=F32)
    for index in range(8):
        rows = placed[index * 32 : index * 32 + CAP]
        wide[:CAP, :], wide[CAP:, :] = rows[:, :256], rows[:, 256:]
        packed = wide[...].astype(BF16)
        for copy in range(4):
            out_ref[index * 4 + copy] = packed


def assemble_kernel(got_ref, out_ref, wide):
    for index in range(32):
        rows = got_ref[index].astype(F32)
        here = pl.ds(index % 4 * CAP, CAP)
        start = index // 4 * 512
        wide[here, start : start + 256] = rows[:CAP]
        wide[here, start + 256 : start + 512] = rows[CAP:]
    out_ref[...] = wide[...].astype(BF16)


def expand_kernel(blocks, pairs, *refs):
    inputs = blocks + 2 * pairs
    sources, outs, refs = refs[:inputs], refs[inputs : inputs + pairs], refs[inputs + pairs :]
    rows, held, made, sems = refs[0], refs[1 : 1 + pairs], refs[1 + pairs : -1], refs[-1]
    copies, start = [], 0
    for source in sources[:blocks]:
        size = source.shape[0]
        copies.append((source, rows.at[pl.ds(start, size)]))
        start += size
    units = made[0].shape[0]
    for index, source in enumerate(sources[blocks:]):
        target = held[index // 2].at[pl.ds(index % 2 * units, units)]
        copies.append((source, target))
    copies = [
        pltpu.make_async_copy(source, target, sems.at[index])
        for index, (source, target) in enumerate(copies)
    ]
    for copy in copies:
        copy.start()
    for copy in copies[:blocks]:
        copy.wait()
    sent = []
    for index, (weight, hidden, out) in enumerate(zip(held, made, outs)):
        for copy in copies[blocks + 2 * index : blocks + 2 * index + 2]:
            copy.wait()
        both = lax.dot_general(
            weight[...], rows[...], (((1,), (1,)), ((), ())), preferred_element_type=F32
        )
        hidden[...] = (silu(both[:units]) * both[units:]).astype(BF16)
        sent.append(pltpu.make_async_copy(hidden, out, sems.at[inputs + index]))
        sent[-1].start()
    for copy in sent:
        copy.wait()


def expand(blocks, pairs, name):
    weights = [weight for pair in pairs for weight in pair]
    units, count = weights[0].shape[0], sum(block.shape[0] for block in blocks)
    out = shape((units, count), BF16)
    total = len(pairs)
    return pl.pallas_call(
        functools.partial(expand_kernel, len(blocks), total),
        out_shape=(out,) * total,
        in_specs=[WHOLE] * (len(blocks) + 2 * total),
        out_specs=(WHOLE,) * total,
        scratch_shapes=[
            pltpu.VMEM((count, 4096), BF16),
            *[pltpu.VMEM((2 * units, 4096), BF16)] * total,
            *[pltpu.VMEM(out.shape, BF16)] * total,
            pltpu.SemaphoreType.DMA((len(blocks) + 3 * total,)),
        ],
        name=name,
        compiler_params=pltpu.CompilerParams(vmem_limit_bytes=60 << 20),
        cost_estimate=pl.CostEstimate(
            flops=4 * total * units * count * 4096, transcendentals=0, bytes_accessed=8 << 20
        ),
    )(*blocks, *weights)


def divided(value, by):
    return (value * (65536 // by + 1)) >> 16


EARLY = ((0, 0), (1, 0), (1, 1), (2, 0), (2, 1))
LATE = ((3, 0), (3, 1), (4, 0))


def last_kernel(place_ref, *refs):
    (*sources, out_ref), held = refs[:9], refs[9:-1]
    rows, weight, mine_early, other_early, other_late, mine_late, out, sems = *held, refs[-1]
    size, units = sources[0].shape[0], sources[3].shape[0]
    targets = [rows.at[pl.ds(index * size, size)] for index in range(3)]
    targets += [weight.at[pl.ds(index * units, units)] for index in range(2)]
    targets += [mine_early, other_early, other_late]
    copies = [
        pltpu.make_async_copy(source, target, sems.at[index])
        for index, (source, target) in enumerate(zip(sources, targets))
    ]
    for copy in copies[5:] + copies[:5]:
        copy.start()

    def ordered(pair, blocks, first):
        count = pair[0].shape[1]
        row = lax.broadcasted_iota(jnp.int32, (count, 1), 0)
        block = divided(row, 4 * CAP)
        within = row - block * (4 * CAP)
        steps, twin = (jnp.full_like(row, value) for value in blocks[0])
        for index, (step, other) in enumerate(blocks[1:], 1):
            steps = jnp.where(block == index, step, steps)
            twin = jnp.where(block == index, other, twin)
        base = within + divided(within, CAP) * CAP
        places = []
        for ref, holder in zip(pair, (place_ref[1], 1 - place_ref[1])):
            layer = (place_ref[0] + steps * (2 * holder - 1)) & 7
            core = holder + twin * (1 - 2 * holder)
            places.append((ref, layer * (8 * CAP) + core * CAP + base))
        for start in range(0, out.shape[1], 256):
            here = slice(start, start + 256)
            total = jnp.zeros((units, 256), F32) if first else out[:, here].astype(F32)
            for ref, target in places:
                column = lax.broadcasted_iota(jnp.int32, (count, 256), 1) + start
                table = jnp.where(column == target, 1.0, 0.0).astype(BF16)
                total = total + jnp.dot(ref[...], table, preferred_element_type=F32)
            out[:, here] = total.astype(BF16)

    for copy in copies[5:7]:
        copy.wait()
    ordered((mine_early, other_early), EARLY, True)
    for copy in copies[7:] + copies[:5]:
        copy.wait()
    both = lax.dot_general(
        weight[...], rows[...], (((1,), (1,)), ((), ())), preferred_element_type=F32
    )
    mine_late[...] = (silu(both[:units]) * both[units:]).astype(BF16)
    ordered((mine_late, other_late), LATE, False)
    copy = pltpu.make_async_copy(out, out_ref, sems.at[0])
    copy.start()
    copy.wait()


def last(place, blocks, pair, mine_early, other_early, other_late):
    units, count = pair[0].shape[0], 3 * blocks[0].shape[0]
    out = shape((units, 1280), BF16)
    return pl.pallas_call(
        last_kernel,
        out_shape=out,
        in_specs=[SMEM] + [WHOLE] * 8,
        out_specs=WHOLE,
        scratch_shapes=[
            pltpu.VMEM((count, 4096), BF16),
            pltpu.VMEM((2 * units, 4096), BF16),
            pltpu.VMEM(mine_early.shape, BF16),
            pltpu.VMEM(other_early.shape, BF16),
            pltpu.VMEM((units, count), BF16),
            pltpu.VMEM((units, count), BF16),
            pltpu.VMEM(out.shape, BF16),
            pltpu.SemaphoreType.DMA((8,)),
        ],
        name="last",
        compiler_params=pltpu.CompilerParams(vmem_limit_bytes=60 << 20),
        cost_estimate=pl.CostEstimate(flops=1 << 30, transcendentals=0, bytes_accessed=8 << 20),
    )(place, *blocks, *pair, mine_early, other_early, other_late)


def silu(value):
    return value / (1.0 + jnp.exp(-value))


def softplus(value):
    small = jnp.exp(-jnp.abs(value))
    ratio = small / (2.0 + small)
    square = ratio * ratio
    series = jnp.full_like(square, 1.0 / 15.0)
    for odd in (13, 11, 9, 7, 5, 3):
        series = series * square + 1.0 / odd
    return jnp.maximum(value, 0.0) + 2.0 * ratio * (series * square + 1.0)


def conv_kernel(
    x_ref,
    rim_ref,
    raw_ref,
    weight_ref,
    proj_ref,
    bias_ref,
    decay_ref,
    conv_ref,
    step_ref,
    drive_ref,
    rate_ref,
    part_ref,
    padded,
):
    rows, width = x_ref.shape
    padded[8:, :] = x_ref[...].astype(F32)
    padded[5:8, :] = rim_ref[...].astype(F32)
    total = jnp.zeros((rows, width), F32)
    for tap in range(4):
        total = total + weight_ref[tap : tap + 1, :] * padded[5 + tap : 5 + tap + rows, :]
    conv = silu(total)
    conv_ref[...] = conv
    part = lax.dot_general(
        proj_ref[...], conv.astype(BF16), (((1,), (1,)), ((), ())), preferred_element_type=F32
    )
    for index in range(8):
        part_ref[index] = part
    step = softplus(raw_ref[...].astype(F32) + bias_ref[...])
    drive = step * conv
    rate = -jnp.exp(decay_ref[...]) * LOG2E
    for index in range(width // 128):
        lanes = slice(index * 128, index * 128 + 128)
        step_ref[pl.ds(index, rows, stride=8), :] = step[:, lanes]
        drive_ref[pl.ds(index, rows, stride=8), :] = drive[:, lanes]
        rate_ref[pl.ds(index, rate.shape[0], stride=8), :] = rate[:, lanes]


def pack_state(states, total):
    high = total.astype(BF16).astype(F32)
    middle = (total - high).astype(BF16).astype(F32)
    low = total - high - middle
    tail = jnp.concatenate([high, middle, low, jnp.zeros_like(total)], axis=0)
    return jnp.concatenate(list(states) + [tail], axis=0).astype(BF16)


def unpack_state(ref, position):
    block = ref[position].astype(F32)
    states = [block[n * 8 : n * 8 + 8] for n in range(16)]
    return states, block[128:136] + block[136:144] + block[144:152]


def scan_kernel(coef_ref, step_ref, drive_ref, rate_ref, y_ref, sum_ref, end_ref):
    rows = step_ref.shape[0] // 8
    rates = [rate_ref[n * 8 : n * 8 + 8, :] for n in range(16)]
    zero = jnp.zeros((8, 128), F32)

    def advance(token, carry):
        total, states = carry
        here = pl.ds(pl.multiple_of(token * 8, 8), 8)
        step, drive = step_ref[here, :], drive_ref[here, :]
        total = total + step
        sum_ref[here, :] = total
        parts, following = [zero, zero], []
        for n in range(16):
            state = jnp.exp2(rates[n] * step) * states[n] + coef_ref[n, token] * drive
            parts[n % 2] = parts[n % 2] + coef_ref[16 + n, token] * state
            following.append(state)
        y_ref[here, :] = parts[0] + parts[1]
        return total, tuple(following)

    total, states = lax.fori_loop(0, rows, advance, (zero, (zero,) * 16), unroll=4)
    packed = pack_state(states, total)
    for index in range(8):
        end_ref[index] = packed


def fold(ref, rates, limit, states, total):
    for position in range(8):
        more, step = unpack_state(ref, position)
        keep = position < limit
        states = [
            jnp.where(keep, jnp.exp2(rates[n] * step) * states[n] + more[n], states[n])
            for n in range(16)
        ]
        total = jnp.where(keep, total + step, total)
    return states, total


def group_kernel(mine_ref, got_ref, rate_ref, before_ref, step_ref, all_ref):
    rates = [rate_ref[n * 8 : n * 8 + 8, :] for n in range(16)]
    zero = jnp.zeros((8, 128), F32)
    states, total = fold(got_ref, rates, mine_ref[0], [zero] * 16, zero)
    for n in range(16):
        before_ref[n * 8 : n * 8 + 8, :] = states[n]
    step_ref[...] = total
    states, total = fold(got_ref, rates, 8, [zero] * 16, zero)
    packed = pack_state(states, total)
    for index in range(8):
        all_ref[index] = packed


def finish_kernel(
    copies,
    mine_ref,
    coef_ref,
    got_ref,
    rate_ref,
    before_ref,
    before_step_ref,
    y_ref,
    sum_ref,
    conv_ref,
    gain_ref,
    z_ref,
    out_ref,
    dense,
):
    rows, width = conv_ref.shape
    for copy in copies[:4]:
        copy.wait()
    rates = [rate_ref[n * 8 : n * 8 + 8, :] for n in range(16)]
    zero = jnp.zeros((8, 128), F32)
    states, _ = fold(got_ref, rates, mine_ref[0], [zero] * 16, zero)
    states = [
        jnp.exp2(rates[n] * before_step_ref[...]) * states[n] + before_ref[n * 8 : n * 8 + 8, :]
        for n in range(16)
    ]

    for copy in copies[4:6]:
        copy.wait()

    def advance(token, carry):
        here = pl.ds(pl.multiple_of(token * 8, 8), 8)
        total = sum_ref[here, :]
        parts = [y_ref[here, :], zero]
        for n in range(16):
            parts[n % 2] = parts[n % 2] + coef_ref[16 + n, token] * (
                jnp.exp2(rates[n] * total) * states[n]
            )
        dense[here, :] = parts[0] + parts[1]
        return carry

    lax.fori_loop(0, rows, advance, 0, unroll=4)
    for copy in copies[6:]:
        copy.wait()
    for index in range(width // 128):
        lanes = slice(index * 128, index * 128 + 128)
        value = dense[pl.ds(index, rows, stride=8), :]
        value = value + gain_ref[:, lanes] * conv_ref[:, lanes]
        out_ref[:, lanes] = (value * silu(z_ref[:, lanes].astype(F32))).astype(BF16)


def shards(
    inner_x,
    inner_z,
    step_raw,
    conv_weight,
    state_proj,
    step_bias,
    decay_log,
    skip_gain,
    moe_tokens,
    routes,
    gate_weight,
    up_weight,
):
    rows, width = inner_x.shape
    shards_of = lax.axis_size(SEQ)
    rim = lax.ppermute(inner_x[rows - 3 :], SEQ, [(i, i + 1) for i in range(shards_of - 1)])
    swap = [(0, 1), (1, 0)]
    features = moe_tokens.shape[1]
    placed = call(
        place_kernel,
        shape((32, 2 * CAP, features // 2), BF16),
        [WHOLE] * 2,
        [pltpu.VMEM((2 * CAP, features // 2), F32)],
        name="place",
        flops=1 << 28,
    )(routes.T, moe_tokens)
    arrived = lax.all_to_all(placed, ("exp", "x"), split_axis=0, concat_axis=0, tiled=True)
    dense = shape((rows * width // 128, 128), F32)
    conv, step, drive, rate, part = call(
        conv_kernel,
        (
            shape((rows, width), F32),
            dense,
            dense,
            shape((128, 128), F32),
            shape((8, 32, rows), F32),
        ),
        [WHOLE] * 7,
        [pltpu.VMEM((rows + 8, width), F32)],
        name="conv", flops=1 << 29,
    )(inner_x, rim, step_raw, conv_weight, state_proj.T, step_bias[None], decay_log)
    dense = shape((rows * width // 128, 128), F32)
    conv, step, drive, rate, part = call(
        conv_kernel,
        (
            shape((rows, width), F32),
            dense,
            dense,
            shape((128, 128), F32),
            shape((8, 32, rows), F32),
        ),
        [WHOLE] * 7,
        [pltpu.VMEM((rows + 8, width), F32)],
        name="conv", flops=1 << 29,
    )(inner_x, rim, step_raw, conv_weight, state_proj.T, step_bias[None], decay_log)
    weight = jnp.concatenate([gate_weight[0], up_weight[0]], axis=0)
    weights = gate_weight[0], up_weight[0]
    others = [lax.ppermute(weight, "c", swap) for weight in weights]
    arrived, part, *others = lax.optimization_barrier((arrived, part, *others))
    pairs = [others, weights]
    block = call(
        assemble_kernel,
        shape((4 * CAP, 4096), BF16),
        [WHOLE],
        [pltpu.VMEM((4 * CAP, 4096), F32)],
        name="assemble",
        vmem=16,
        flops=1 << 28,
    )(arrived)
    onward = [(2 * z + c, 2 * ((z + 1 - 2 * c) % 8) + c) for z in range(8) for c in range(2)]

    def step_on(rows):
        return lax.ppermute(rows, ("z", "c"), onward)

    own, twin = [block, step_on(block)], [lax.ppermute(block, "c", swap)]
    twin[0], part = lax.optimization_barrier((twin[0], part))
    twin.append(step_on(twin[0]))
    coef = lax.all_to_all(part, "exp", split_axis=0, concat_axis=0, tiled=True)
    own[1], coef = lax.optimization_barrier((own[1], coef))
    coef = jnp.sum(coef, axis=0)
    packed = shape((8, 160, 128), BF16)
    local, sums, ends = call(
        scan_kernel, (dense, dense, packed), [SMEM] + [WHOLE] * 3, name="scan", flops=1 << 31
    )(coef, step, drive, rate)
    own.append(step_on(own[1]))
    twin.append(step_on(twin[1]))
    own[2], _ = lax.optimization_barrier((own[2], ends))
    own.append(step_on(own[2]))
    twin.append(step_on(twin[2]))
    other_early, mine_early = expand([block, own[1], twin[1], own[2], twin[2]], pairs, "expand_early")
    own[3], _ = lax.optimization_barrier((own[3], other_early))
    own.append(step_on(own[3]))
    near = lax.all_to_all(ends, ("x", "c"), split_axis=0, concat_axis=0, tiled=True)
    place_in = lax.axis_index(("x", "c")).astype(jnp.int32).reshape(1)
    before, before_step, whole = call(
        group_kernel,
        (shape((128, 128), F32), shape((8, 128), F32), packed),
        [SMEM, WHOLE, WHOLE],
        name="group", vmem=16, flops=1 << 28,
    )(place_in, near, rate)
    far = lax.all_to_all(whole, "z", split_axis=0, concat_axis=0, tiled=True)
    layer = lax.axis_index("z").astype(jnp.int32).reshape(1)
    mixed = call(
        finish_kernel,
        shape((rows, width), BF16),
        [SMEM, SMEM] + [WHOLE] * 9,
        [pltpu.VMEM(dense.shape, F32)],
        lazy=True, name="finish", flops=1 << 31,
    )(layer, coef, far, rate, before, before_step, local, sums, conv, skip_gain[None], inner_z)

    late = [own[3], twin[3], own[4]]
    (other_late,) = expand(late, pairs[:1], "expand_other")
    other_early, other_late = (lax.ppermute(part, "c", swap) for part in (other_early, other_late))
    here = jnp.stack([lax.axis_index("z"), lax.axis_index("c")]).astype(jnp.int32)
    other_late, mixed = lax.optimization_barrier((other_late, mixed))
    hidden = last(here, late, weights, mine_early, other_early, other_late)[None]
    return mixed, hidden


def solution(mesh):
    fine = Mesh(mesh.devices.reshape(8, 4, 2, 8), ("z", "x", "c", "exp"))
    return jax.shard_map(
        shards,
        mesh=fine,
        in_specs=(
            P(SEQ, "exp"),
            P(SEQ, "exp"),
            P(SEQ, "exp"),
            P(None, "exp"),
            P("exp", None),
            P("exp"),
            P(None, "exp"),
            P("exp"),
            P(SEQ, "exp"),
            P(SEQ, None),
            P("exp", SEQ, None),
            P("exp", SEQ, None),
        ),
        out_specs=(P(SEQ, "exp"), P("exp", SEQ, None)),
        check_vma=False,
    )
```
